32 devices in a mesh: pair: 8 (over y, x, core), row: 4 (over z).
Axes of the slice: x: 2, y: 2, z: 4, core: 2. Of those that a mesh axis runs over, the one named last changes fastest.
Arguments:
- amplitudes: bfloat16 [3, 160, 32, 5120], P(None, 'pair', 'row'), may hold values from -6 to 6
- integrals: bfloat16 [3, 5120, 5120], P(None, 'row', 'pair'), may hold values from -0.078125 to 0.078125
- occupied_irrep: int32 [32], replicated, may hold values from 0 to 7
- virtual_order: int32 [1280], replicated, may hold values from 0 to 1279, each once
- block_irreps: int32 [3], replicated, may hold values from 0 to 7
- occupied_energy: float32 [32], replicated, may hold values from -2 to -0.5
- virtual_energy: float32 [1280], replicated, may hold values from 1 to 4
Outputs:
- update: float32 [3, 160, 32, 5120], P(None, None, 'row', 'pair')
The draws below stay inside these ranges and needn't reach their ends.
Inputs may be any that keep to these rules, and one draw needn't show every extreme that they name: virtual_order holds every virtual orbital once; entries g * 160 to g * 160 + 159 are the virtual orbitals of irrep g.
All inputs are finite; a program needn't handle non-finite values.
Results may differ from the reference program's by a relative error of at most 0.0003.
Values may be sent and summed in bfloat16 or wider, within the bound.
A program may use at most 128 MiB of HBM per device.

```python
import jax
import jax.numpy as jnp

NO = 32
VIRG = 160
IRREPS = 8
IRR = 3
NV = 1280
P_SIZE = 5120


def touch_ends(values, own_key, smallest, high):
    place = [jax.random.randint(jax.random.fold_in(own_key, axis), (), 0, length) for axis, length in enumerate(values.shape)]
    longest = values.shape.index(max(values.shape))
    neighbour = place[:longest] + [(place[longest] + 1) % values.shape[longest]] + place[longest + 1:]
    return values.at[tuple(place)].set(smallest).at[tuple(neighbour)].set(high)


def block_scale(rng, shape, pieces, low, high):
    gain = 1.0
    for dim, parts in pieces:
        draws = jax.random.uniform(jax.random.fold_in(jax.random.fold_in(rng, 6), dim), (parts,), jnp.float32, low / len(pieces), high / len(pieces))
        gain = gain * jnp.repeat(jnp.exp(draws), shape[dim] // parts).reshape((-1,) + (1,) * (len(shape) - 1 - dim))
    return gain


def scatter_about(own_key, dims, spread, reach, shards=(), kind=jnp.bfloat16):
    entries = spread * jax.random.normal(own_key, dims, jnp.float32)
    if shards:
        entries = entries * block_scale(own_key, dims, shards, -0.22, 0.18)
    return jnp.clip(entries, -reach, reach).astype(kind)


def setup_inputs(seed: int = 0) -> dict:
    splits = jax.random.split(jax.random.key(seed), 8)
    amplitudes = scatter_about(splits[0], (IRR, VIRG, NO, P_SIZE), 1.0, 6.0, ((1, 8), (2, 4)))
    integrals = scatter_about(splits[1], (IRR, P_SIZE, P_SIZE), P_SIZE ** -0.5, 0.078125, ((1, 4), (2, 8)))
    occupied_irrep = touch_ends(jax.random.randint(splits[2], (NO,), 0, IRREPS), jax.random.fold_in(splits[2], 1), 0, IRREPS - 1).astype(jnp.int32)
    virtual_order = jax.random.permutation(splits[3], NV).astype(jnp.int32)
    block_irreps = jax.random.randint(splits[4], (IRR,), 0, IRREPS).astype(jnp.int32)
    occupied_energy = jnp.clip(jax.random.uniform(splits[5], (NO,), jnp.float32, -2.0, -0.5), -2.0, -0.5)
    virtual_energy = jnp.clip(jax.random.uniform(splits[6], (NV,), jnp.float32, 1.0, 4.0), 1.0, 4.0)
    return {"amplitudes": amplitudes, "integrals": integrals, "occupied_irrep": occupied_irrep, "virtual_order": virtual_order, "block_irreps": block_irreps, "occupied_energy": occupied_energy, "virtual_energy": virtual_energy}


def shift_table(occupied_irrep, virtual_order, block_irreps, occupied_energy, virtual_energy):
    pair_irrep = jnp.bitwise_xor(block_irreps[:, None], occupied_irrep[None, :]).astype(jnp.int32)
    orbital_slot = pair_irrep[:, None, :] * VIRG + jnp.arange(VIRG, dtype=jnp.int32)[None, :, None]
    orbital_index = jnp.take(virtual_order, orbital_slot.astype(jnp.int32))
    return jnp.take(virtual_energy, orbital_index) - occupied_energy[None, None, :]


def reference(amplitudes, integrals, occupied_irrep, virtual_order, block_irreps, occupied_energy, virtual_energy):
    shift = shift_table(occupied_irrep, virtual_order, block_irreps, occupied_energy, virtual_energy)
    results = []
    for irrep_block in range(IRR):
        matrix = amplitudes[irrep_block].reshape(VIRG * NO, P_SIZE)
        cycle_term = jnp.dot(matrix, integrals[irrep_block], preferred_element_type=jnp.float32)
        flat_shift = shift[irrep_block].reshape(VIRG * NO)
        denominator = flat_shift[:, None] + flat_shift[None, :]
        results.append((cycle_term / denominator).reshape(VIRG, NO, P_SIZE))
    return jnp.stack(results)
```

```python
import jax
import jax.numpy as jnp
from jax import lax
from jax.experimental import pallas as pl
from jax.experimental.pallas import tpu as pltpu
from jax.sharding import PartitionSpec as P

VIRG = 160


def shift_table(occupied_irrep, virtual_order, block_irreps, occupied_energy, virtual_energy):
    count_virt = virtual_energy.shape[0]
    orbital_ids = jnp.arange(count_virt, dtype=jnp.int32)
    matches = virtual_order[:, None] == orbital_ids[None, :]
    slot_energy = jnp.sum(jnp.where(matches, virtual_energy[None, :], jnp.float32(0.0)), axis=1)
    irrep_count = count_virt // VIRG
    energy_grid = slot_energy.reshape(irrep_count, VIRG)
    pair_irrep = jnp.bitwise_xor(block_irreps[:, None], occupied_irrep[None, :])
    irrep_ids = jnp.arange(irrep_count, dtype=jnp.int32)
    chosen = pair_irrep[:, None, None, :] == irrep_ids[None, :, None, None]
    picked = jnp.sum(jnp.where(chosen, energy_grid[None, :, :, None], jnp.float32(0.0)), axis=1)
    return picked - occupied_energy[None, None, :]


def body(
    amplitudes,
    integrals,
    occupied_irrep,
    virtual_order,
    block_irreps,
    occupied_energy,
    virtual_energy,
):
    block_count, virt_local, occ_local, pair_width = amplitudes.shape
    column_width = integrals.shape[2]
    shift = shift_table(
        occupied_irrep, virtual_order, block_irreps, occupied_energy, virtual_energy
    )
    occ_start = lax.axis_index("row") * occ_local
    col_start = lax.axis_index("pair") * column_width
    results = []
    for block in range(block_count):
        whole_rows = lax.all_gather(integrals[block], "row", axis=0, tiled=True)
        piece = lax.all_gather(amplitudes[block], "pair", axis=0, tiled=True)
        flat = piece.reshape(piece.shape[0] * piece.shape[1], piece.shape[2])
        product = jnp.dot(flat, whole_rows, preferred_element_type=jnp.float32)
        cycle_term = product.reshape(piece.shape[0], piece.shape[1], whole_rows.shape[1])
        row_shift = lax.dynamic_slice_in_dim(shift[block], occ_start, occ_local, 1)
        col_shift = lax.dynamic_slice_in_dim(
            shift[block].reshape(pair_width), col_start, column_width, 0
        )
        denominator = row_shift[:, :, None] + col_shift[None, None, :]
        results.append(cycle_term / denominator)
    return jnp.stack(results)


HALVES = 2
TILE = 320
GROUPS = 8
HELPED, FIRST, LAST = 0, 1, 2
EXTRA = 3
MID = [(FIRST, "own"), (HELPED, "own"), (FIRST, "near"), (HELPED, "near"), (LAST, "own"), (LAST, "near")]
OUT = [(FIRST, "own"), (FIRST, "mid"), (LAST, "own"), (FIRST, "far"), (LAST, "mid"), (LAST, "far")]
IN = [(FIRST, "own"), (HELPED, "own"), (LAST, "own")]
MESH = pl.DeviceIdType.MESH


def encode(total, coded_ref, scale_ref):
    group = TILE // GROUPS
    for part in range(GROUPS // 2):
        words = []
        for place in (part, part + GROUPS // 2):
            values = total[place * group : (place + 1) * group]
            top = jnp.maximum(jnp.max(jnp.abs(values), axis=0, keepdims=True), jnp.float32(1e-33))
            scale_ref[place : place + 1, :] = top * jnp.float32(1.0 / 32767.0)
            words.append(jnp.round(values * (jnp.float32(32767.0) / top)).astype(jnp.int32))
        coded_ref[part * group : (part + 1) * group, :] = (words[0] << 16) | (words[1] & 0xFFFF)


def decode(coded_ref, scale_ref, out_ref):
    group = TILE // GROUPS
    for part in range(GROUPS // 2):
        words = coded_ref[part * group : (part + 1) * group, :]
        for place, values in ((part, words >> 16), (part + GROUPS // 2, (words << 16) >> 16)):
            out_ref[place * group : (place + 1) * group, :] = (
                values.astype(jnp.float32) * scale_ref[place : place + 1, :]
            )


def kernel(
    a_ref, b_ref, cycle_ref, all_a, all_b, partial, held, coded, scales,
    mid_send, mid_recv, out_send, out_recv, in_send, in_recv, p_send, p_recv, own_sem,
):
    blocks, a_rows, _ = a_ref.shape
    b_rows = b_ref.shape[1]
    pair = lax.axis_index("pair")
    row = lax.axis_index("row")
    near = row ^ 1
    across = 3 - row
    far = across ^ 1
    is_inner = (row == 1) | (row == 2)

    barrier = pltpu.get_barrier_semaphore()
    friends = [(pair, near), (pair, across)] + [(pair ^ step, row) for step in (1, 2, 4)]
    for friend in friends:
        pl.semaphore_signal(barrier, inc=1, device_id=friend, device_id_type=MESH)
    pl.semaphore_wait(barrier, len(friends))

    def remote(source, goal, send, recv, place, device):
        return pltpu.make_async_remote_copy(
            src_ref=source,
            dst_ref=goal,
            send_sem=send.at[place],
            recv_sem=recv.at[place],
            device_id=device,
            device_id_type=MESH,
        )

    def piece(half, rows):
        size = rows // HALVES
        return pl.ds(half * size, size)

    def mid_copy(index):
        block, kind = MID[index // HALVES]
        part = piece(index % HALVES, b_rows)
        slot = row if kind == "own" else near
        source = b_ref.at[block, part] if kind == "own" else all_b.at[block, near, part]
        return remote(source, all_b.at[block, slot, part], mid_send, mid_recv, index, (pair, across))

    def out_copy(index):
        block, kind = OUT[index // HALVES]
        part = piece(index % HALVES, b_rows)
        slot = {"own": row, "mid": across, "far": far}[kind]
        source = b_ref.at[block, part] if kind == "own" else all_b.at[block, slot, part]
        return remote(source, all_b.at[block, slot, part], out_send, out_recv, index, (pair, near))

    def coded_copies():
        count = HALVES * len(OUT)
        return [
            remote(coded, coded, out_send, out_recv, count, (pair, near)),
            remote(scales, scales, out_send, out_recv, count + 1, (pair, near)),
        ]

    def in_copy(index):
        if index < HALVES:
            part = piece(index, a_rows)
            source, goal = a_ref.at[HELPED, part], all_a.at[EXTRA, pair, part]
        else:
            block = IN[index // HALVES - 1][0]
            part = piece(index % HALVES, b_rows)
            source, goal = b_ref.at[block, part], all_b.at[block, row, part]
        return remote(source, goal, in_send, in_recv, index, (pair, near))

    in_count = HALVES * (1 + len(IN))

    def own_part(which):
        return all_a.at[EXTRA, pair] if which == EXTRA else a_ref.at[which]

    def plane_copy(which, step, half):
        part = piece(half, a_rows)
        return remote(
            own_part(which).at[part],
            all_a.at[which, pair, part],
            p_send,
            p_recv,
            10 * which + 2 * (step - 1) + half,
            (pair ^ (2 * step), row),
        )

    def forward_copy(which, step):
        part = piece(step - 1, a_rows)
        owner = pair ^ (2 * step)
        return remote(
            all_a.at[which, owner, part],
            all_a.at[which, owner, part],
            p_send,
            p_recv,
            10 * which + 3 + step,
            (pair ^ (6 - 2 * step), row),
        )

    def core_copy(which, step):
        owner = pair ^ (2 * step)
        return remote(
            own_part(which) if step == 0 else all_a.at[which, owner],
            all_a.at[which, owner],
            p_send,
            p_recv,
            10 * which + 6 + step,
            (pair ^ 1, row),
        )

    def gather_start(which):
        plane_copy(which, 1, 0).start()
        plane_copy(which, 2, 1).start()
        plane_copy(which, 1, 1).start()
        plane_copy(which, 2, 0).start()
        core_copy(which, 0).start()

    def gather_forward(which):
        plane_copy(which, 1, 0).wait_recv()
        forward_copy(which, 1).start()
        plane_copy(which, 2, 1).wait_recv()
        forward_copy(which, 2).start()

    def gather_share(which):
        for step in (1, 2):
            plane_copy(which, step, 2 - step).wait_recv()
            core_copy(which, step).start()

    def gather_corner(which):
        for step in (1, 2):
            forward_copy(which, step).wait_recv()
        core_copy(which, 3).start()

    def gather_done(which):
        for step in range(4):
            core_copy(which, step).wait_recv()

    def gather_sent(which):
        for step in (1, 2):
            for half in range(HALVES):
                plane_copy(which, step, half).wait_send()
            forward_copy(which, step).wait_send()
        for step in range(4):
            core_copy(which, step).wait_send()

    def own_load(block):
        return pltpu.make_async_copy(a_ref.at[block], held.at[block], own_sem.at[0, block])

    def own_store(block):
        return pltpu.make_async_copy(held.at[block], all_a.at[block, pair], own_sem.at[1, block])

    def own_b(block):
        return pltpu.make_async_copy(b_ref.at[block], all_b.at[block, row], own_sem.at[2, block])

    def multiply(which, block, first, parts, goal=None, begin=None, keep=False, code=False):
        count, rows, _ = all_a.shape[1:]
        depth, columns = all_b.shape[2:]

        def tile(a_tile, *rest):
            def add(part, total):
                start = pl.multiple_of(part * depth, depth)
                left = a_tile[:, :, pl.ds(start, depth)].reshape(TILE, depth)
                return total + jnp.dot(
                    left, all_b[block, first + part], preferred_element_type=jnp.float32
                )

            at = pl.program_id(0)
            total = jnp.zeros((TILE, columns), jnp.float32) if begin is None else begin[at]
            total = lax.fori_loop(0, parts, add, total)
            if code:
                encode(total, coded.at[at], scales.at[at])
            elif keep:
                partial[at] = total
            else:
                rest[0][...] = total

        start = pl.multiple_of(first * depth, depth)
        pltpu.emit_pipeline(
            tile,
            grid=(count * rows // TILE,),
            in_specs=[pl.BlockSpec((TILE // rows, rows, parts * depth), lambda i: (i, 0, 0))],
            out_specs=[] if goal is None else [pl.BlockSpec((TILE, columns), lambda i: (i, 0))],
        )(all_a.at[which, :, :, pl.ds(start, parts * depth)], *([] if goal is None else [goal]))

    def unpack(goal):
        def tile(out_tile):
            at = pl.program_id(0)
            decode(coded.at[at], scales.at[at], out_tile)

        pltpu.emit_pipeline(
            tile,
            grid=(coded.shape[0],),
            out_specs=[pl.BlockSpec((TILE, goal.shape[1]), lambda i: (i, 0))],
        )(goal)

    low, high = row // 2, 3 * (1 - row // 2)

    @pl.when(is_inner)
    def _():
        def arrive(step):
            mid_copy(step).wait_recv()
            later = step + 2
            if later < HALVES * len(MID):
                block, kind = MID[later // HALVES]
                if kind == "near":
                    place = HALVES * (1 + [entry[0] for entry in IN].index(block)) + later % HALVES
                    in_copy(place).wait_recv()
                mid_copy(later).start()
            block, kind = MID[step // HALVES]
            entry = (block, "mid" if kind == "own" else "far")
            if entry in OUT:
                out_copy(HALVES * OUT.index(entry) + step % HALVES).start()

        for half in range(HALVES):
            mid_copy(half).start()
            out_copy(half).start()
        gather_start(FIRST)
        for block in range(blocks):
            own_load(block).start()
            own_b(block).start()
        for block in range(blocks):
            own_load(block).wait()
            own_store(block).start()
        arrive(0)
        gather_forward(FIRST)
        arrive(1)
        gather_share(FIRST)
        for half in range(HALVES):
            in_copy(half).wait_recv()
        gather_start(EXTRA)
        arrive(2)
        out_copy(2 * HALVES).start()
        gather_corner(FIRST)
        arrive(3)
        out_copy(2 * HALVES + 1).start()
        gather_forward(EXTRA)
        arrive(4)
        gather_share(EXTRA)
        gather_start(HELPED)
        arrive(5)
        gather_corner(EXTRA)
        own_store(FIRST).wait()
        own_b(FIRST).wait()
        gather_done(FIRST)
        multiply(FIRST, FIRST, 0, 4, cycle_ref.at[FIRST])
        gather_forward(HELPED)
        arrive(6)
        own_b(HELPED).wait()
        gather_done(EXTRA)
        multiply(EXTRA, HELPED, low, 3, keep=True)
        arrive(7)
        multiply(EXTRA, HELPED, high, 1, begin=partial, code=True)
        for copy in coded_copies():
            copy.start()
        gather_share(HELPED)
        gather_start(LAST)
        arrive(8)
        gather_corner(HELPED)
        arrive(9)
        own_store(HELPED).wait()
        gather_done(HELPED)
        multiply(HELPED, HELPED, 0, 4, cycle_ref.at[HELPED])
        gather_forward(LAST)
        arrive(10)
        gather_share(LAST)
        arrive(11)
        gather_corner(LAST)
        own_store(LAST).wait()
        own_b(LAST).wait()
        gather_done(LAST)
        multiply(LAST, LAST, 0, 4, cycle_ref.at[LAST])
        for index in range(HALVES * len(MID)):
            mid_copy(index).wait_send()
        for index in range(HALVES * len(OUT)):
            out_copy(index).wait_send()
        for copy in coded_copies():
            copy.wait_send()
        for which in (FIRST, EXTRA, HELPED, LAST):
            gather_sent(which)

    @pl.when(jnp.logical_not(is_inner))
    def _():
        def arrive(step):
            out_copy(step).wait_recv()
            if step + 2 < in_count:
                in_copy(step + 2).start()

        for half in range(HALVES):
            in_copy(half).start()
        gather_start(FIRST)
        for block in (FIRST, LAST):
            own_load(block).start()
            own_b(block).start()
        for block in (FIRST, LAST):
            own_load(block).wait()
            own_store(block).start()
        arrive(0)
        gather_forward(FIRST)
        arrive(1)
        gather_share(FIRST)
        gather_start(LAST)
        arrive(2)
        gather_corner(FIRST)
        arrive(3)
        gather_forward(LAST)
        arrive(4)
        gather_share(LAST)
        arrive(5)
        gather_corner(LAST)
        arrive(6)
        arrive(7)
        own_store(FIRST).wait()
        own_b(FIRST).wait()
        gather_done(FIRST)
        multiply(FIRST, FIRST, 0, 4, cycle_ref.at[FIRST])
        for copy in coded_copies():
            copy.wait_recv()
        unpack(cycle_ref.at[HELPED])
        arrive(8)
        arrive(9)
        own_store(LAST).wait()
        own_b(LAST).wait()
        gather_done(LAST)
        multiply(LAST, LAST, low, 3, keep=True)
        arrive(10)
        arrive(11)
        multiply(LAST, LAST, high, 1, cycle_ref.at[LAST], partial)
        for index in range(in_count):
            in_copy(index).wait_send()
        for which in (FIRST, LAST):
            gather_sent(which)


def linked_body(
    amplitudes,
    integrals,
    occupied_irrep,
    virtual_order,
    block_irreps,
    occupied_energy,
    virtual_energy,
):
    blocks, virt_local, occ_local, pair_width = amplitudes.shape
    depth, column_width = integrals.shape[1:]
    rows = virt_local * occ_local
    shift = shift_table(
        occupied_irrep, virtual_order, block_irreps, occupied_energy, virtual_energy
    )
    row_shift = lax.dynamic_slice_in_dim(shift, lax.axis_index("row") * occ_local, occ_local, 2)
    col_shift = lax.dynamic_slice_in_dim(
        shift.reshape(blocks, pair_width), lax.axis_index("pair") * column_width, column_width, 1
    )
    cycle_term = pl.pallas_call(
        kernel,
        out_shape=(
            jax.ShapeDtypeStruct((blocks, 8 * rows, column_width), jnp.float32),
            jax.ShapeDtypeStruct((blocks + 1, 8, rows, pair_width), jnp.bfloat16),
        ),
        in_specs=[pl.BlockSpec(memory_space=pl.ANY)] * 2,
        out_specs=(pl.BlockSpec(memory_space=pl.ANY),) * 2,
        scratch_shapes=[
            pltpu.VMEM((blocks, 4, depth, column_width), jnp.bfloat16),
            pltpu.VMEM((8 * rows // TILE, TILE, column_width), jnp.float32),
            pltpu.VMEM((blocks, rows, pair_width), jnp.bfloat16),
            pltpu.VMEM((8 * rows // TILE, TILE // 2, column_width), jnp.int32),
            pltpu.VMEM((8 * rows // TILE, GROUPS, column_width), jnp.float32),
            pltpu.SemaphoreType.DMA((HALVES * len(MID),)),
            pltpu.SemaphoreType.DMA((HALVES * len(MID),)),
            pltpu.SemaphoreType.DMA((HALVES * len(OUT) + 2,)),
            pltpu.SemaphoreType.DMA((HALVES * len(OUT) + 2,)),
            pltpu.SemaphoreType.DMA((HALVES * (1 + len(IN)),)),
            pltpu.SemaphoreType.DMA((HALVES * (1 + len(IN)),)),
            pltpu.SemaphoreType.DMA((10 * (blocks + 1),)),
            pltpu.SemaphoreType.DMA((10 * (blocks + 1),)),
            pltpu.SemaphoreType.DMA((3, blocks)),
        ],
        compiler_params=pltpu.CompilerParams(
            collective_id=0, has_side_effects=True, vmem_limit_bytes=50 * 2**20
        ),
    )(amplitudes.reshape(blocks, rows, pair_width), integrals)[0]
    cycle_term = cycle_term.reshape(blocks, 8 * virt_local, occ_local, column_width)
    return cycle_term / (row_shift[..., None] + col_shift[:, None, None, :])


def solution(mesh):
    placed = (P(None, "pair", "row", None), P(None, "row", "pair"), P(), P(), P(), P(), P())
    linked = mesh.shape["pair"] == 8 and mesh.shape["row"] == 4
    return jax.shard_map(
        linked_body if linked else body,
        mesh=mesh,
        in_specs=placed,
        out_specs=P(None, None, "row", "pair"),
        check_vma=False,
    )
```

```python
import jax
import jax.numpy as jnp
from jax import lax
from jax.experimental import pallas as pl
from jax.experimental.pallas import tpu as pltpu
from jax.sharding import PartitionSpec as P

VIRG = 160


def shift_table(occupied_irrep, virtual_order, block_irreps, occupied_energy, virtual_energy):
    count_virt = virtual_energy.shape[0]
    orbital_ids = jnp.arange(count_virt, dtype=jnp.int32)
    matches = virtual_order[:, None] == orbital_ids[None, :]
    slot_energy = jnp.sum(jnp.where(matches, virtual_energy[None, :], jnp.float32(0.0)), axis=1)
    irrep_count = count_virt // VIRG
    energy_grid = slot_energy.reshape(irrep_count, VIRG)
    pair_irrep = jnp.bitwise_xor(block_irreps[:, None], occupied_irrep[None, :])
    irrep_ids = jnp.arange(irrep_count, dtype=jnp.int32)
    chosen = pair_irrep[:, None, None, :] == irrep_ids[None, :, None, None]
    picked = jnp.sum(jnp.where(chosen, energy_grid[None, :, :, None], jnp.float32(0.0)), axis=1)
    return picked - occupied_energy[None, None, :]


def body(
    amplitudes,
    integrals,
    occupied_irrep,
    virtual_order,
    block_irreps,
    occupied_energy,
    virtual_energy,
):
    block_count, virt_local, occ_local, pair_width = amplitudes.shape
    column_width = integrals.shape[2]
    shift = shift_table(
        occupied_irrep, virtual_order, block_irreps, occupied_energy, virtual_energy
    )
    occ_start = lax.axis_index("row") * occ_local
    col_start = lax.axis_index("pair") * column_width
    results = []
    for block in range(block_count):
        whole_rows = lax.all_gather(integrals[block], "row", axis=0, tiled=True)
        piece = lax.all_gather(amplitudes[block], "pair", axis=0, tiled=True)
        flat = piece.reshape(piece.shape[0] * piece.shape[1], piece.shape[2])
        product = jnp.dot(flat, whole_rows, preferred_element_type=jnp.float32)
        cycle_term = product.reshape(piece.shape[0], piece.shape[1], whole_rows.shape[1])
        row_shift = lax.dynamic_slice_in_dim(shift[block], occ_start, occ_local, 1)
        col_shift = lax.dynamic_slice_in_dim(
            shift[block].reshape(pair_width), col_start, column_width, 0
        )
        denominator = row_shift[:, :, None] + col_shift[None, None, :]
        results.append(cycle_term / denominator)
    return jnp.stack(results)


CHUNKS = 4
HALVES = 2
TILE = 320
GROUPS = 8
HELPED, FIRST, LAST = 0, 1, 2
EXTRA = 3
MID = [(FIRST, "own"), (HELPED, "own"), (FIRST, "near"), (HELPED, "near"), (LAST, "own"), (LAST, "near")]
OUT = [(FIRST, "own"), (FIRST, "mid"), (LAST, "own"), (FIRST, "far"), (LAST, "mid"), (LAST, "far")]
IN = [FIRST, HELPED, LAST]
MESH = pl.DeviceIdType.MESH


def encode(total, coded_ref, scale_ref):
    group = TILE // GROUPS
    for part in range(GROUPS // 2):
        words = []
        for place in (part, part + GROUPS // 2):
            values = total[place * group : (place + 1) * group]
            top = jnp.maximum(jnp.max(jnp.abs(values), axis=0, keepdims=True), jnp.float32(1e-33))
            scale_ref[place : place + 1, :] = top * jnp.float32(1.0 / 32767.0)
            words.append(jnp.round(values * (jnp.float32(32767.0) / top)).astype(jnp.int32))
        coded_ref[part * group : (part + 1) * group, :] = (words[0] << 16) | (words[1] & 0xFFFF)


def decode(coded_ref, scale_ref, row_shift, col_shift, out_ref):
    group = TILE // GROUPS
    for part in range(GROUPS // 2):
        words = coded_ref[part * group : (part + 1) * group, :]
        for place, values in ((part, words >> 16), (part + GROUPS // 2, (words << 16) >> 16)):
            inside = slice(place * group, (place + 1) * group)
            total = values.astype(jnp.float32) * scale_ref[place : place + 1, :]
            out_ref[inside, :] = total / (row_shift[inside, :] + col_shift)


def kernel(
    a_ref, b_ref, irrep_ref, order_ref, block_ref, occupied_ref, virtual_ref, out_ref, all_a,
    all_b, tiles, tail, coded, scales, row_ref, col_ref,
    mid_send, mid_recv, out_send, out_recv, code_send, code_recv, in_send, in_recv, p_send, p_recv,
    own_sem, tile_sem, tail_sem,
):
    blocks, a_rows, _ = a_ref.shape
    depth, columns = b_ref.shape[1:]
    chunk, half_depth = depth // CHUNKS, depth // HALVES
    pieces = all_a.shape[1]
    group = TILE // a_rows
    count = pieces // group
    pair = lax.axis_index("pair")
    row = lax.axis_index("row")
    near = row ^ 1
    across = 3 - row
    far = across ^ 1
    is_inner = (row == 1) | (row == 2)

    barrier = pltpu.get_barrier_semaphore()
    friends = [(pair, near), (pair, across)] + [(pair ^ step, row) for step in (1, 2, 4)]
    for friend in friends:
        pl.semaphore_signal(barrier, inc=1, device_id=friend, device_id_type=MESH)
    pl.semaphore_wait(barrier, len(friends))

    def remote(source, goal, send, recv, place, device):
        return pltpu.make_async_remote_copy(
            src_ref=source,
            dst_ref=goal,
            send_sem=send.at[place],
            recv_sem=recv.at[place],
            device_id=device,
            device_id_type=MESH,
        )

    def b_copy(block, slot, turn, own, send, recv, place, device):
        offset = jnp.where(slot == 0, CHUNKS - 1 - turn, turn) * chunk
        goal = all_b.at[block, pl.ds(pl.multiple_of(slot * depth + offset, chunk), chunk)]
        source = b_ref.at[block, pl.ds(pl.multiple_of(offset, chunk), chunk)] if own else goal
        return remote(source, goal, send, recv, place, device)

    def mid_copy(index):
        block, kind = MID[index // CHUNKS]
        slot = row if kind == "own" else near
        return b_copy(
            block, slot, index % CHUNKS, kind == "own", mid_send, mid_recv, index, (pair, across)
        )

    def out_copy(index):
        block, kind = OUT[index // CHUNKS]
        slot = {"own": row, "mid": across, "far": far}[kind]
        return b_copy(
            block, slot, index % CHUNKS, kind == "own", out_send, out_recv, index, (pair, near)
        )

    def in_copy(index):
        return b_copy(
            IN[index // CHUNKS], row, index % CHUNKS, True, in_send, in_recv, index, (pair, near)
        )

    def code_copies(at):
        return [
            remote(coded.at[at], coded.at[at], code_send, code_recv, 2 * at, (pair, near)),
            remote(scales.at[at], scales.at[at], code_send, code_recv, 2 * at + 1, (pair, near)),
        ]

    def piece(half):
        size = a_rows // HALVES
        return pl.ds(half * size, size)

    def extra_copy(half):
        part = piece(half)
        return remote(
            a_ref.at[HELPED, part],
            all_a.at[EXTRA, pair, part],
            in_send,
            in_recv,
            CHUNKS * len(IN) + half,
            (pair, near),
        )

    def own_part(which):
        return all_a.at[EXTRA, pair] if which == EXTRA else a_ref.at[which]

    def plane_copy(which, step, half):
        part = piece(half)
        return remote(
            own_part(which).at[part],
            all_a.at[which, pair, part],
            p_send,
            p_recv,
            10 * which + 2 * (step - 1) + half,
            (pair ^ (2 * step), row),
        )

    def forward_copy(which, step):
        part = piece(step - 1)
        owner = pair ^ (2 * step)
        return remote(
            all_a.at[which, owner, part],
            all_a.at[which, owner, part],
            p_send,
            p_recv,
            10 * which + 3 + step,
            (pair ^ (6 - 2 * step), row),
        )

    def core_copy(which, step):
        owner = pair ^ (2 * step)
        return remote(
            own_part(which) if step == 0 else all_a.at[which, owner],
            all_a.at[which, owner],
            p_send,
            p_recv,
            10 * which + 6 + step,
            (pair ^ 1, row),
        )

    def gather_start(which):
        plane_copy(which, 1, 0).start()
        plane_copy(which, 2, 1).start()
        plane_copy(which, 1, 1).start()
        plane_copy(which, 2, 0).start()
        core_copy(which, 0).start()

    def gather_forward(which):
        plane_copy(which, 1, 0).wait_recv()
        forward_copy(which, 1).start()
        plane_copy(which, 2, 1).wait_recv()
        forward_copy(which, 2).start()

    def gather_share(which):
        for step in (1, 2):
            plane_copy(which, step, 2 - step).wait_recv()
            core_copy(which, step).start()

    def gather_corner(which):
        for step in (1, 2):
            forward_copy(which, step).wait_recv()
        core_copy(which, 3).start()

    def gather_done(which):
        for step in range(4):
            core_copy(which, step).wait_recv()

    def gather_sent(which):
        for step in (1, 2):
            for half in range(HALVES):
                plane_copy(which, step, half).wait_send()
            forward_copy(which, step).wait_send()
        for step in range(4):
            core_copy(which, step).wait_send()

    def own_b(block):
        return pltpu.make_async_copy(
            b_ref.at[block],
            all_b.at[block, pl.ds(pl.multiple_of(row * depth, depth), depth)],
            own_sem.at[block],
        )

    def fill_shifts():
        count_virt = order_ref.shape[0]
        lanes = 128

        def iota(shape, dim):
            return lax.broadcasted_iota(jnp.int32, shape, dim)

        def pick(match, values, axis):
            chosen = jnp.where(match, values, jnp.float32(0.0))
            return jnp.sum(chosen, axis=axis, keepdims=True)

        def upright(line):
            same = iota((lanes, lanes), 0) == iota((lanes, lanes), 1)
            return jnp.concatenate(
                [
                    pick(same, line[:, start : start + lanes], 1)
                    for start in range(0, count_virt, lanes)
                ],
                axis=0,
            )

        def spread(index, scalars):
            chosen = jnp.full(index.shape, scalars[0])
            for place, scalar in enumerate(scalars[1:], 1):
                chosen = jnp.where(index == place, scalar, chosen)
            return chosen

        energies = upright(virtual_ref[...].reshape(1, count_virt))
        order = order_ref[...].reshape(1, count_virt)
        line = jnp.zeros((1, count_virt), jnp.float32)
        for start in range(0, count_virt, lanes):
            match = iota((lanes, count_virt), 0) + start == order
            line += pick(match, energies[start : start + lanes], 0)
        stand = upright(line)
        occ_local = irrep_ref.shape[0] // 4
        place = iota((1, columns), 1)
        which = lax.rem(place, irrep_ref.shape[0])
        irreps = spread(which, [irrep_ref[i] for i in range(irrep_ref.shape[0])])
        occupied = spread(which, [occupied_ref[i] for i in range(irrep_ref.shape[0])])
        virt = place // irrep_ref.shape[0] + pair * (columns // irrep_ref.shape[0])
        for block in range(blocks):
            goal = (irreps ^ block_ref[block]) * VIRG + virt
            total = jnp.zeros((1, columns), jnp.float32)
            for start in range(0, count_virt, 2 * lanes):
                match = iota((2 * lanes, columns), 0) + start == goal
                total += pick(match, stand[start : start + 2 * lanes], 0)
            col_ref[block] = total - occupied

        place = iota((lanes, 1), 0)
        which = lax.rem(place, occ_local)
        irreps = spread(which, [irrep_ref[row * occ_local + i] for i in range(occ_local)])
        occupied = spread(which, [occupied_ref[row * occ_local + i] for i in range(occ_local)])

        def strip(turn, carry):
            start = pl.multiple_of(turn * lanes, lanes)
            for block in range(blocks):
                goal = (irreps ^ block_ref[block]) * VIRG + (place + start) // occ_local
                match = iota((lanes, count_virt), 1) == goal
                row_ref[block, pl.ds(start, lanes), :] = pick(match, line, 1) - occupied
            return carry

        lax.fori_loop(0, row_ref.shape[1] // lanes, strip, 0)

    low, high = row // 2, 3 * (1 - row // 2)
    early = pl.multiple_of(high * depth + jnp.where(high == 0, half_depth, 0), half_depth)
    late = pl.multiple_of(high * depth + jnp.where(high == 0, 0, half_depth), half_depth)

    def fetch(which, owner, goal, sem, span=None):
        def start(source):
            source = source if span is None else source.at[:, span]
            pltpu.make_async_copy(source, goal, sem).start()

        if which == EXTRA:
            start(all_a.at[which, owner])
        else:

            @pl.when(owner == pair)
            def _():
                start(a_ref.at[which])

            @pl.when(owner != pair)
            def _():
                start(all_a.at[which, owner])

    def tile_load(which, at, slot):
        for place in range(group):
            fetch(which, at * group + place, tiles.at[slot, place], tile_sem.at[slot, place])

    def tail_load(which):
        for owner in range(pieces):
            fetch(which, owner, tail.at[owner], tail_sem.at[owner], pl.ds(late, half_depth))

    def tail_wait(which):
        for owner in range(pieces):
            pltpu.make_async_copy(
                all_a.at[which, owner, :, pl.ds(late, half_depth)], tail.at[owner], tail_sem.at[owner]
            ).wait()

    def product(left, block, start, size):
        right = all_b[block, pl.ds(start, size), :]
        return jnp.dot(left.reshape(TILE, size), right, preferred_element_type=jnp.float32)

    def divide(total, block, place):
        return total / (row_ref[block, place, :] + col_ref[block])

    def multiply(which, block, first, parts, rest=False):
        tile_load(which, 0, 0)

        def step(at, carry):
            slot = at % 2

            @pl.when(at + 1 < count)
            def _():
                tile_load(which, at + 1, 1 - slot)

            for place in range(group):
                pltpu.make_async_copy(
                    all_a.at[which, at * group + place], tiles.at[slot, place], tile_sem.at[slot, place]
                ).wait()

            def add(part, total):
                start = pl.multiple_of((first + part) * depth, depth)
                return total + product(tiles[slot, :, :, pl.ds(start, depth)], block, start, depth)

            total = lax.fori_loop(0, parts, add, jnp.zeros((TILE, columns), jnp.float32))
            if rest:
                total += product(tiles[slot, :, :, pl.ds(early, half_depth)], block, early, half_depth)
            place = pl.ds(pl.multiple_of(at * TILE, TILE), TILE)
            out_ref[block, place, :] = total if rest else divide(total, block, place)
            return carry

        lax.fori_loop(0, count, step, 0)

    def finish(block, code):
        def step(at, carry):
            place = pl.ds(pl.multiple_of(at * TILE, TILE), TILE)
            left = tail[pl.ds(at * group, group)]
            total = out_ref[block, place, :] + product(left, block, late, half_depth)
            if code:
                encode(total, coded.at[at], scales.at[at])
                for copy in code_copies(at):
                    copy.start()
            else:
                out_ref[block, place, :] = divide(total, block, place)
            return carry

        lax.fori_loop(0, count, step, 0)

    @pl.when(is_inner)
    def _():
        def arrive(turn):
            for step in range(turn * CHUNKS // 2, (turn + 1) * CHUNKS // 2):
                mid_copy(step).wait_recv()
                block, kind = MID[step // CHUNKS]
                entry = (block, "mid" if kind == "own" else "far")
                if entry in OUT:
                    out_copy(CHUNKS * OUT.index(entry) + step % CHUNKS).start()
                later = step + CHUNKS
                if later < CHUNKS * len(MID):
                    block, kind = MID[later // CHUNKS]
                    if kind == "near":
                        in_copy(CHUNKS * IN.index(block) + later % CHUNKS).wait_recv()
                    mid_copy(later).start()

        def fill(block, half):
            for step in range(half * CHUNKS // 2, (half + 1) * CHUNKS // 2):
                out_copy(CHUNKS * OUT.index((block, "own")) + step).start()

        for step in range(CHUNKS):
            mid_copy(step).start()
            out_copy(step).start()
        gather_start(FIRST)
        for block in (FIRST, HELPED, LAST):
            own_b(block).start()
        fill_shifts()
        arrive(0)
        gather_forward(FIRST)
        arrive(1)
        gather_share(FIRST)
        for half in range(HALVES):
            extra_copy(half).wait_recv()
        gather_start(EXTRA)
        arrive(2)
        fill(LAST, 0)
        gather_corner(FIRST)
        arrive(3)
        fill(LAST, 1)
        gather_forward(EXTRA)
        arrive(4)
        gather_share(EXTRA)
        gather_start(HELPED)
        arrive(5)
        gather_corner(EXTRA)
        own_b(FIRST).wait()
        gather_done(FIRST)
        multiply(FIRST, FIRST, 0, 4)
        gather_forward(HELPED)
        arrive(6)
        own_b(HELPED).wait()
        gather_done(EXTRA)
        tail_load(EXTRA)
        multiply(EXTRA, HELPED, low, 3, True)
        tail_wait(EXTRA)
        arrive(7)
        finish(HELPED, True)
        gather_share(HELPED)
        gather_start(LAST)
        arrive(8)
        gather_corner(HELPED)
        arrive(9)
        gather_done(HELPED)
        multiply(HELPED, HELPED, 0, 4)
        gather_forward(LAST)
        arrive(10)
        gather_share(LAST)
        arrive(11)
        gather_corner(LAST)
        own_b(LAST).wait()
        gather_done(LAST)
        multiply(LAST, LAST, 0, 4)
        for index in range(CHUNKS * len(MID)):
            mid_copy(index).wait_send()
        for index in range(CHUNKS * len(OUT)):
            out_copy(index).wait_send()
        for at in range(count):
            for copy in code_copies(at):
                copy.wait_send()
        for which in (FIRST, EXTRA, HELPED, LAST):
            gather_sent(which)

    @pl.when(jnp.logical_not(is_inner))
    def _():
        def arrive(turn):
            for step in range(turn * CHUNKS // 2, (turn + 1) * CHUNKS // 2):
                out_copy(step).wait_recv()
                if step < CHUNKS * len(IN):
                    in_copy(step).start()

        for half in range(HALVES):
            extra_copy(half).start()
        gather_start(FIRST)
        for block in (FIRST, LAST):
            own_b(block).start()
        fill_shifts()
        arrive(0)
        gather_forward(FIRST)
        arrive(1)
        gather_share(FIRST)
        gather_start(LAST)
        arrive(2)
        gather_corner(FIRST)
        arrive(3)
        gather_forward(LAST)
        arrive(4)
        gather_share(LAST)
        arrive(5)
        gather_corner(LAST)
        arrive(6)
        arrive(7)
        own_b(FIRST).wait()
        gather_done(FIRST)
        multiply(FIRST, FIRST, 0, 4)
        own_b(LAST).wait()
        gather_done(LAST)
        tail_load(LAST)
        for at in range(count):
            for copy in code_copies(at):
                copy.wait_recv()
            place = pl.ds(at * TILE, TILE)
            decode(
                coded.at[at],
                scales.at[at],
                row_ref[HELPED, place, :],
                col_ref[HELPED],
                out_ref.at[HELPED, place],
            )
        tail_wait(LAST)
        arrive(8)
        arrive(9)
        arrive(10)
        multiply(LAST, LAST, low, 3, True)
        arrive(11)
        finish(LAST, False)
        for half in range(HALVES):
            extra_copy(half).wait_send()
        for index in range(CHUNKS * len(IN)):
            in_copy(index).wait_send()
        for which in (FIRST, LAST):
            gather_sent(which)


def linked_body(
    amplitudes,
    integrals,
    occupied_irrep,
    virtual_order,
    block_irreps,
    occupied_energy,
    virtual_energy,
):
    blocks, virt_local, occ_local, pair_width = amplitudes.shape
    depth, column_width = integrals.shape[1:]
    rows = virt_local * occ_local
    update = pl.pallas_call(
        kernel,
        out_shape=(
            pltpu.VMEM((blocks, 8 * rows, column_width), jnp.float32),
            jax.ShapeDtypeStruct((blocks + 1, 8, rows, pair_width), jnp.bfloat16),
        ),
        in_specs=[pl.BlockSpec(memory_space=pl.ANY)] * 2
        + [
            pl.BlockSpec(memory_space=pltpu.SMEM),
            pl.BlockSpec(memory_space=pltpu.VMEM),
            pl.BlockSpec(memory_space=pltpu.SMEM),
            pl.BlockSpec(memory_space=pltpu.SMEM),
            pl.BlockSpec(memory_space=pltpu.VMEM),
        ],
        out_specs=(pl.BlockSpec(memory_space=pltpu.VMEM), pl.BlockSpec(memory_space=pl.ANY)),
        scratch_shapes=[
            pltpu.VMEM((blocks, pair_width, column_width), jnp.bfloat16),
            pltpu.VMEM((2, TILE // rows, rows, pair_width), jnp.bfloat16),
            pltpu.VMEM((8, rows, depth // HALVES), jnp.bfloat16),
            pltpu.VMEM((8 * rows // TILE, TILE // 2, column_width), jnp.int32),
            pltpu.VMEM((8 * rows // TILE, GROUPS, column_width), jnp.float32),
            pltpu.VMEM((blocks, 8 * rows, 1), jnp.float32),
            pltpu.VMEM((blocks, 1, column_width), jnp.float32),
            pltpu.SemaphoreType.DMA((CHUNKS * len(MID),)),
            pltpu.SemaphoreType.DMA((CHUNKS * len(MID),)),
            pltpu.SemaphoreType.DMA((CHUNKS * len(OUT),)),
            pltpu.SemaphoreType.DMA((CHUNKS * len(OUT),)),
            pltpu.SemaphoreType.DMA((2 * 8 * rows // TILE,)),
            pltpu.SemaphoreType.DMA((2 * 8 * rows // TILE,)),
            pltpu.SemaphoreType.DMA((CHUNKS * len(IN) + HALVES,)),
            pltpu.SemaphoreType.DMA((CHUNKS * len(IN) + HALVES,)),
            pltpu.SemaphoreType.DMA((10 * (blocks + 1),)),
            pltpu.SemaphoreType.DMA((10 * (blocks + 1),)),
            pltpu.SemaphoreType.DMA((blocks,)),
            pltpu.SemaphoreType.DMA((2, TILE // rows)),
            pltpu.SemaphoreType.DMA((8,)),
        ],
        compiler_params=pltpu.CompilerParams(
            collective_id=0, has_side_effects=True, vmem_limit_bytes=46 * 2**20
        ),
    )(
        amplitudes.reshape(blocks, rows, pair_width),
        integrals,
        occupied_irrep,
        virtual_order,
        block_irreps,
        occupied_energy,
        virtual_energy,
    )[0]
    return update.reshape(blocks, 8 * virt_local, occ_local, column_width)


def solution(mesh):
    placed = (P(None, "pair", "row", None), P(None, "row", "pair"), P(), P(), P(), P(), P())
    linked = mesh.shape["pair"] == 8 and mesh.shape["row"] == 4
    return jax.shard_map(
        linked_body if linked else body,
        mesh=mesh,
        in_specs=placed,
        out_specs=P(None, None, "row", "pair"),
        check_vma=False,
    )
```

```python
import jax
import jax.numpy as jnp
from jax import lax
from jax.experimental import pallas as pl
from jax.experimental.pallas import tpu as pltpu
from jax.sharding import PartitionSpec as P

VIRG = 160


def shift_table(occupied_irrep, virtual_order, block_irreps, occupied_energy, virtual_energy):
    count_virt = virtual_energy.shape[0]
    orbital_ids = jnp.arange(count_virt, dtype=jnp.int32)
    matches = virtual_order[:, None] == orbital_ids[None, :]
    slot_energy = jnp.sum(jnp.where(matches, virtual_energy[None, :], jnp.float32(0.0)), axis=1)
    irrep_count = count_virt // VIRG
    energy_grid = slot_energy.reshape(irrep_count, VIRG)
    pair_irrep = jnp.bitwise_xor(block_irreps[:, None], occupied_irrep[None, :])
    irrep_ids = jnp.arange(irrep_count, dtype=jnp.int32)
    chosen = pair_irrep[:, None, None, :] == irrep_ids[None, :, None, None]
    picked = jnp.sum(jnp.where(chosen, energy_grid[None, :, :, None], jnp.float32(0.0)), axis=1)
    return picked - occupied_energy[None, None, :]


def body(
    amplitudes,
    integrals,
    occupied_irrep,
    virtual_order,
    block_irreps,
    occupied_energy,
    virtual_energy,
):
    block_count, virt_local, occ_local, pair_width = amplitudes.shape
    column_width = integrals.shape[2]
    shift = shift_table(
        occupied_irrep, virtual_order, block_irreps, occupied_energy, virtual_energy
    )
    occ_start = lax.axis_index("row") * occ_local
    col_start = lax.axis_index("pair") * column_width
    results = []
    for block in range(block_count):
        whole_rows = lax.all_gather(integrals[block], "row", axis=0, tiled=True)
        piece = lax.all_gather(amplitudes[block], "pair", axis=0, tiled=True)
        flat = piece.reshape(piece.shape[0] * piece.shape[1], piece.shape[2])
        product = jnp.dot(flat, whole_rows, preferred_element_type=jnp.float32)
        cycle_term = product.reshape(piece.shape[0], piece.shape[1], whole_rows.shape[1])
        row_shift = lax.dynamic_slice_in_dim(shift[block], occ_start, occ_local, 1)
        col_shift = lax.dynamic_slice_in_dim(
            shift[block].reshape(pair_width), col_start, column_width, 0
        )
        denominator = row_shift[:, :, None] + col_shift[None, None, :]
        results.append(cycle_term / denominator)
    return jnp.stack(results)


CHUNKS = 4
HALVES = 2
TILE = 320
GROUPS = 8
HELPED, FIRST, LAST = 0, 1, 2
EXTRA, SHARED = 3, 4
KEPT = 512
MID = [(LAST, "own"), (HELPED, "own"), (HELPED, "near"), (FIRST, "own"), (FIRST, "near"), (LAST, "near")]
OUT = [(LAST, "own"), (LAST, "mid"), (FIRST, "own"), (FIRST, "mid"), (FIRST, "far"), (LAST, "far")]
IN = [HELPED, FIRST, LAST]
MESH = pl.DeviceIdType.MESH


def encode(total, coded_ref, scale_ref):
    group = TILE // GROUPS
    for part in range(GROUPS // 2):
        words = []
        for place in (part, part + GROUPS // 2):
            values = total[place * group : (place + 1) * group]
            top = jnp.maximum(jnp.max(jnp.abs(values), axis=0, keepdims=True), jnp.float32(1e-33))
            scale_ref[place : place + 1, :] = top * jnp.float32(1.0 / 32767.0)
            words.append(jnp.round(values * (jnp.float32(32767.0) / top)).astype(jnp.int32))
        coded_ref[part * group : (part + 1) * group, :] = (words[0] << 16) | (words[1] & 0xFFFF)


def decode(coded_ref, scale_ref, row_shift, col_shift, out_ref):
    group = TILE // GROUPS
    for part in range(GROUPS // 2):
        words = coded_ref[part * group : (part + 1) * group, :]
        for place, values in ((part, words >> 16), (part + GROUPS // 2, (words << 16) >> 16)):
            inside = slice(place * group, (place + 1) * group)
            total = values.astype(jnp.float32) * scale_ref[place : place + 1, :]
            out_ref[inside, :] = total / (row_shift[inside, :] + col_shift)


def kernel(
    a_ref, b_ref, irrep_ref, order_ref, block_ref, occupied_ref, virtual_ref, out_ref, all_a,
    all_b, tiles, tail, coded, scales, row_ref, col_ref, aside,
    beside, shared, shared_scales,
    mid_send, mid_recv, out_send, out_recv, code_send, code_recv, in_send, in_recv, p_send, p_recv,
    own_sem, tile_sem, tail_sem, beside_send, beside_recv, shared_send, shared_recv,
):
    blocks, a_rows, _ = a_ref.shape
    depth, columns = b_ref.shape[1:]
    chunk, half_depth = depth // CHUNKS, depth // HALVES
    pieces = all_a.shape[1]
    group = TILE // a_rows
    count = pieces // group
    pair = lax.axis_index("pair")
    row = lax.axis_index("row")
    near = row ^ 1
    across = 3 - row
    far = across ^ 1
    is_inner = (row == 1) | (row == 2)

    barrier = pltpu.get_barrier_semaphore()
    friends = [(pair, near), (pair ^ 2, near), (pair, across)] + [(pair ^ step, row) for step in (1, 2, 4)]
    for friend in friends:
        pl.semaphore_signal(barrier, inc=1, device_id=friend, device_id_type=MESH)
    pl.semaphore_wait(barrier, len(friends))

    def remote(source, goal, send, recv, place, device):
        return pltpu.make_async_remote_copy(
            src_ref=source,
            dst_ref=goal,
            send_sem=send.at[place],
            recv_sem=recv.at[place],
            device_id=device,
            device_id_type=MESH,
        )

    def b_copy(block, slot, turn, own, send, recv, place, device, width=columns):
        kept = pl.ds(0, width)
        offset = jnp.where(slot == 0, CHUNKS - 1 - turn, turn) * chunk
        goal = all_b.at[block, pl.ds(pl.multiple_of(slot * depth + offset, chunk), chunk), kept]
        source = b_ref.at[block, pl.ds(pl.multiple_of(offset, chunk), chunk), kept] if own else goal
        return remote(source, goal, send, recv, place, device)

    def mid_copy(index):
        block, kind = MID[index // CHUNKS]
        slot = row if kind == "own" else near
        return b_copy(
            block, slot, index % CHUNKS, kind == "own", mid_send, mid_recv, index, (pair, across)
        )

    def out_copy(index):
        block, kind = OUT[index // CHUNKS]
        slot = {"own": row, "mid": across, "far": far}[kind]
        return b_copy(
            block, slot, index % CHUNKS, kind == "own", out_send, out_recv, index, (pair, near),
            KEPT if block == FIRST else columns,
        )

    def in_copy(index):
        return b_copy(
            IN[index // CHUNKS], row, index % CHUNKS, True, in_send, in_recv, index, (pair, near)
        )

    def code_copies(at):
        return [
            remote(coded.at[at], coded.at[at], code_send, code_recv, 2 * at, (pair, near)),
            remote(scales.at[at], scales.at[at], code_send, code_recv, 2 * at + 1, (pair, near)),
        ]

    def piece(half):
        size = a_rows // HALVES
        return pl.ds(half * size, size)

    def extra_copy(half):
        part = piece(half)
        return remote(
            a_ref.at[HELPED, part],
            all_a.at[EXTRA, pair, part],
            in_send,
            in_recv,
            CHUNKS * len(IN) + half,
            (pair, near),
        )

    def shared_copy(step, half):
        part = piece(half)
        owner = pair ^ (4 * step)
        source = a_ref.at[FIRST, part] if step == 0 else all_a.at[FIRST, owner, part]
        return remote(
            source,
            all_a.at[SHARED, owner, part],
            in_send,
            in_recv,
            CHUNKS * len(IN) + HALVES * (1 + step) + half,
            (pair, near),
        )

    def shared_core(step):
        owner = pair ^ (4 * step)
        source = all_a.at[SHARED, owner]
        return remote(source, source, p_send, p_recv, 10 * SHARED + step, (pair ^ 1, row))

    def beside_copy(slot, place):
        part = pl.ds(pl.multiple_of(slot * depth, depth), depth)
        return remote(aside.at[part], beside.at[part], beside_send, beside_recv, place, (pair ^ 2, row))

    def beside_start(slot, place):
        part = pl.ds(pl.multiple_of(slot * depth, depth), depth)
        aside[part, :] = all_b[FIRST, part, KEPT:]
        beside_copy(slot, place).start()

    def shared_codes(at, turn, side):
        device = (pair ^ (2 * side), near)
        return [
            pltpu.make_async_remote_copy(
                src_ref=held.at[at, side],
                dst_ref=held.at[at, 0],
                send_sem=shared_send.at[4 * turn + 2 * side + place],
                recv_sem=shared_recv.at[2 * at + place],
                device_id=device,
                device_id_type=MESH,
            )
            for place, held in enumerate((shared, shared_scales))
        ]

    def own_part(which):
        return all_a.at[EXTRA, pair] if which == EXTRA else a_ref.at[which]

    def plane_copy(which, step, half):
        part = piece(half)
        return remote(
            own_part(which).at[part],
            all_a.at[which, pair, part],
            p_send,
            p_recv,
            10 * which + 2 * (step - 1) + half,
            (pair ^ (2 * step), row),
        )

    def forward_copy(which, step):
        part = piece(step - 1)
        bit = 2 if which == LAST else 2 * step
        return remote(
            all_a.at[which, pair ^ bit, part],
            all_a.at[which, pair ^ bit, part],
            p_send,
            p_recv,
            10 * which + 3 + step,
            (pair ^ (6 - bit), row),
        )

    def core_copy(which, step):
        owner = pair ^ (2 * step)
        return remote(
            own_part(which) if step == 0 else all_a.at[which, owner],
            all_a.at[which, owner],
            p_send,
            p_recv,
            10 * which + 6 + step,
            (pair ^ 1, row),
        )

    def gather_start(which):
        plane_copy(which, 1, 0).start()
        plane_copy(which, 2, 1).start()
        plane_copy(which, 1, 1).start()
        plane_copy(which, 2, 0).start()
        core_copy(which, 0).start()

    def gather_forward(which):
        plane_copy(which, 1, 0).wait_recv()
        forward_copy(which, 1).start()
        plane_copy(which, 1 if which == LAST else 2, 1).wait_recv()
        forward_copy(which, 2).start()

    def gather_share(which):
        if which == LAST:
            core_copy(which, 1).start()
            for half in range(HALVES):
                plane_copy(which, 2, half).wait_recv()
            core_copy(which, 2).start()
            return
        for step in (1, 2):
            plane_copy(which, step, 2 - step).wait_recv()
            core_copy(which, step).start()

    def gather_corner(which):
        for step in (1, 2):
            forward_copy(which, step).wait_recv()
        core_copy(which, 3).start()

    def gather_done(which, steps=(0, 1, 2, 3)):
        for step in steps:
            core_copy(which, step).wait_recv()

    def gather_sent(which):
        for step in (1, 2):
            for half in range(HALVES):
                plane_copy(which, step, half).wait_send()
            forward_copy(which, step).wait_send()
        for step in range(4):
            core_copy(which, step).wait_send()

    def own_b(block):
        return pltpu.make_async_copy(
            b_ref.at[block],
            all_b.at[block, pl.ds(pl.multiple_of(row * depth, depth), depth)],
            own_sem.at[block],
        )

    def fill_shifts():
        count_virt = order_ref.shape[0]
        lanes = 128

        def iota(shape, dim):
            return lax.broadcasted_iota(jnp.int32, shape, dim)

        def pick(match, values, axis):
            chosen = jnp.where(match, values, jnp.float32(0.0))
            return jnp.sum(chosen, axis=axis, keepdims=True)

        def upright(line):
            same = iota((lanes, lanes), 0) == iota((lanes, lanes), 1)
            return jnp.concatenate(
                [
                    pick(same, line[:, start : start + lanes], 1)
                    for start in range(0, count_virt, lanes)
                ],
                axis=0,
            )

        def spread(index, scalars):
            chosen = jnp.full(index.shape, scalars[0])
            for place, scalar in enumerate(scalars[1:], 1):
                chosen = jnp.where(index == place, scalar, chosen)
            return chosen

        energies = upright(virtual_ref[...].reshape(1, count_virt))
        order = order_ref[...].reshape(1, count_virt)
        line = jnp.zeros((1, count_virt), jnp.float32)
        for start in range(0, count_virt, lanes):
            match = iota((lanes, count_virt), 0) + start == order
            line += pick(match, energies[start : start + lanes], 0)
        stand = upright(line)
        occ_local = irrep_ref.shape[0] // 4
        place = iota((1, columns), 1)
        which = lax.rem(place, irrep_ref.shape[0])
        irreps = spread(which, [irrep_ref[i] for i in range(irrep_ref.shape[0])])
        occupied = spread(which, [occupied_ref[i] for i in range(irrep_ref.shape[0])])
        virt = place // irrep_ref.shape[0] + pair * (columns // irrep_ref.shape[0])
        for block in range(blocks):
            goal = (irreps ^ block_ref[block]) * VIRG + virt
            total = jnp.zeros((1, columns), jnp.float32)
            for start in range(0, count_virt, 2 * lanes):
                match = iota((2 * lanes, columns), 0) + start == goal
                total += pick(match, stand[start : start + 2 * lanes], 0)
            col_ref[block] = total - occupied

        place = iota((lanes, 1), 0)
        which = lax.rem(place, occ_local)
        irreps = spread(which, [irrep_ref[row * occ_local + i] for i in range(occ_local)])
        occupied = spread(which, [occupied_ref[row * occ_local + i] for i in range(occ_local)])

        def strip(turn, carry):
            start = pl.multiple_of(turn * lanes, lanes)
            for block in range(blocks):
                goal = (irreps ^ block_ref[block]) * VIRG + (place + start) // occ_local
                match = iota((lanes, count_virt), 1) == goal
                row_ref[block, pl.ds(start, lanes), :] = pick(match, line, 1) - occupied
            return carry

        lax.fori_loop(0, row_ref.shape[1] // lanes, strip, 0)

    low, high = row // 2, 3 * (1 - row // 2)
    early = pl.multiple_of(high * depth + jnp.where(high == 0, half_depth, 0), half_depth)
    late = pl.multiple_of(high * depth + jnp.where(high == 0, 0, half_depth), half_depth)

    def fetch(which, owner, goal, sem, span=None):
        def start(source):
            source = source if span is None else source.at[:, span]
            pltpu.make_async_copy(source, goal, sem).start()

        if which >= EXTRA:
            start(all_a.at[which, owner])
        else:

            @pl.when(owner == pair)
            def _():
                start(a_ref.at[which])

            @pl.when(owner != pair)
            def _():
                start(all_a.at[which, owner])

    def tile_load(which, at, slot):
        for place in range(group):
            fetch(which, at * group + place, tiles.at[slot, place], tile_sem.at[slot, place])

    def tail_load(which, first, size):
        for owner in range(pieces):
            goal = tail.at[owner, :, pl.ds(0, size)]
            fetch(which, owner, goal, tail_sem.at[owner], pl.ds(first, size))

    def tail_wait(which, first, size):
        for owner in range(pieces):
            goal = tail.at[owner, :, pl.ds(0, size)]
            pltpu.make_async_copy(
                all_a.at[which, owner, :, pl.ds(first, size)], goal, tail_sem.at[owner]
            ).wait()

    def product(left, block, start, size, width=columns):
        right = all_b[block, pl.ds(start, size), :width]
        return jnp.dot(left.reshape(TILE, size), right, preferred_element_type=jnp.float32)

    def divide(total, block, place):
        return total / (row_ref[block, place, :] + col_ref[block][:, : total.shape[1]])

    def share(at, turn):
        tile_load(SHARED, at, 0)
        for place in range(group):
            pltpu.make_async_copy(
                all_a.at[SHARED, at * group + place], tiles.at[0, place], tile_sem.at[0, place]
            ).wait()
        for side in range(2):

            def add(part, total):
                span = pl.ds(pl.multiple_of(part * depth, depth), depth)
                right = beside[span, :] if side else aside[span, :]
                left = tiles[0, :, :, span].reshape(TILE, depth)
                return total + jnp.dot(left, right, preferred_element_type=jnp.float32)

            total = lax.fori_loop(0, 4, add, jnp.zeros((TILE, columns - KEPT), jnp.float32))
            encode(total, shared.at[at, side], shared_scales.at[at, side])
            for copy in shared_codes(at, turn, side):
                copy.start()

    def multiply(which, block, first, parts, rest=False, width=columns, span=(0, count), raw=False):
        home = pair // group
        tile_load(which, home ^ span[0], span[0] % 2)

        def step(turn, carry):
            slot = turn % 2
            at = home ^ turn

            @pl.when(turn + 1 < span[1])
            def _():
                tile_load(which, home ^ (turn + 1), 1 - slot)

            for place in range(group):
                pltpu.make_async_copy(
                    all_a.at[which, at * group + place], tiles.at[slot, place], tile_sem.at[slot, place]
                ).wait()

            def add(part, total):
                start = pl.multiple_of((first + part) * depth, depth)
                return total + product(
                    tiles[slot, :, :, pl.ds(start, depth)], block, start, depth, width
                )

            total = lax.fori_loop(0, parts, add, jnp.zeros((TILE, width), jnp.float32))
            if rest:
                total += product(tiles[slot, :, :, pl.ds(early, half_depth)], block, early, half_depth)
            place = pl.ds(pl.multiple_of(at * TILE, TILE), TILE)
            out_ref[block, place, :width] = total if raw else divide(total, block, place)
            return carry

        lax.fori_loop(span[0], span[1], step, 0)

    def finish(block, code, first, size):
        def step(at, carry):
            place = pl.ds(pl.multiple_of(at * TILE, TILE), TILE)
            left = tail[pl.ds(at * group, group), :, :size]
            total = out_ref[block, place, :] + product(left, block, first, size)
            if code:
                encode(total, coded.at[at], scales.at[at])
                for copy in code_copies(at):
                    copy.start()
            else:
                out_ref[block, place, :] = divide(total, block, place)
            return carry

        lax.fori_loop(0, count, step, 0)

    @pl.when(is_inner)
    def _():
        def arrive(turn):
            for step in range(turn * CHUNKS // 2, (turn + 1) * CHUNKS // 2):
                mid_copy(step).wait_recv()
                block, kind = MID[step // CHUNKS]
                entry = (block, "mid" if kind == "own" else "far")
                if entry in OUT:
                    out_copy(CHUNKS * OUT.index(entry) + step % CHUNKS).start()
                later = step + CHUNKS
                if later < CHUNKS * len(MID):
                    block, kind = MID[later // CHUNKS]
                    if kind == "near":
                        in_copy(CHUNKS * IN.index(block) + later % CHUNKS).wait_recv()
                    mid_copy(later).start()

        def fill(block, half):
            for step in range(half * CHUNKS // 2, (half + 1) * CHUNKS // 2):
                out_copy(CHUNKS * OUT.index((block, "own")) + step).start()

        for step in range(CHUNKS):
            mid_copy(step).start()
            out_copy(step).start()
        gather_start(HELPED)
        for block in (HELPED, FIRST, LAST):
            own_b(block).start()
        fill_shifts()
        arrive(0)
        arrive(1)
        for half in range(HALVES):
            extra_copy(half).wait_recv()
        gather_start(EXTRA)
        fill(FIRST, 0)
        arrive(2)
        fill(FIRST, 1)
        own_b(FIRST).wait()
        beside_start(row, 0)
        arrive(3)
        gather_forward(EXTRA)
        gather_forward(HELPED)
        gather_share(EXTRA)
        gather_share(HELPED)
        gather_start(FIRST)
        own_b(HELPED).wait()
        gather_done(EXTRA, (0, 1, 2))
        multiply(EXTRA, HELPED, low, 3, span=(0, 3), raw=True)
        arrive(4)
        gather_corner(EXTRA)
        gather_done(EXTRA, (3,))
        begin = pl.multiple_of(high * depth, depth)
        tail_load(EXTRA, begin, depth)
        multiply(EXTRA, HELPED, low, 3, span=(3, 4), raw=True)
        tail_wait(EXTRA, begin, depth)
        arrive(5)
        finish(HELPED, True, begin, depth)
        gather_corner(HELPED)
        arrive(6)
        gather_forward(FIRST)
        gather_start(LAST)
        gather_done(HELPED)
        multiply(HELPED, HELPED, 0, 4)
        arrive(7)
        gather_share(FIRST)
        beside_start(near, 1)
        beside_start(across, 2)
        arrive(8)
        gather_corner(FIRST)
        arrive(9)
        beside_start(far, 3)
        gather_done(FIRST)
        multiply(FIRST, FIRST, 0, 4)
        gather_forward(LAST)
        arrive(10)
        gather_share(LAST)
        for half in range(HALVES):
            shared_copy(0, half).wait_recv()
        shared_core(0).start()
        own_b(LAST).wait()
        gather_done(LAST, (0, 1, 2))
        multiply(LAST, LAST, low, 3, True, span=(0, 3), raw=True)
        arrive(11)
        for place in range(4):
            beside_copy(row, place).wait_recv()
        shared_core(0).wait_recv()
        share(pair // group, 0)
        for half in range(HALVES):
            shared_copy(1, half).wait_recv()
        shared_core(1).start()
        gather_corner(LAST)
        gather_done(LAST, (3,))
        tail_load(LAST, late, half_depth)
        shared_core(1).wait_recv()
        share((pair ^ 4) // group, 1)
        multiply(LAST, LAST, low, 3, True, span=(3, 4), raw=True)
        tail_wait(LAST, late, half_depth)
        finish(LAST, False, late, half_depth)
        for index in range(CHUNKS * len(MID)):
            mid_copy(index).wait_send()
        for index in range(CHUNKS * len(OUT)):
            out_copy(index).wait_send()
        for at in range(count):
            for copy in code_copies(at):
                copy.wait_send()
        for which in (FIRST, EXTRA, HELPED, LAST):
            gather_sent(which)
        for step in range(2):
            shared_core(step).wait_send()
            for side in range(2):
                for copy in shared_codes((pair ^ (4 * step)) // group, step, side):
                    copy.wait_send()
        for place, slot in enumerate((row, near, across, far)):
            beside_copy(slot, place).wait_send()

    @pl.when(jnp.logical_not(is_inner))
    def _():
        def arrive(turn):
            for step in range(turn * CHUNKS // 2, (turn + 1) * CHUNKS // 2):
                out_copy(step).wait_recv()
                if step < CHUNKS * len(IN):
                    in_copy(step).start()

        for half in range(HALVES):
            extra_copy(half).start()
        gather_start(FIRST)
        for block in (FIRST, LAST):
            own_b(block).start()
        fill_shifts()
        arrive(0)
        gather_forward(FIRST)
        arrive(1)
        gather_share(FIRST)
        gather_start(LAST)
        arrive(2)
        gather_corner(FIRST)
        arrive(3)
        gather_forward(LAST)
        arrive(4)
        gather_share(LAST)
        arrive(5)
        gather_corner(LAST)
        for at in range(count):
            for copy in code_copies(at):
                copy.wait_recv()
            if at < HALVES:
                shared_copy(0, at).start()
            place = pl.ds(at * TILE, TILE)
            decode(
                coded.at[at],
                scales.at[at],
                row_ref[HELPED, place, :],
                col_ref[HELPED],
                out_ref.at[HELPED, place],
            )
        arrive(6)
        shared_copy(1, 0).start()
        arrive(7)
        shared_copy(1, 1).start()
        arrive(8)
        arrive(9)
        own_b(FIRST).wait()
        gather_done(FIRST)
        multiply(FIRST, FIRST, 0, 4, width=KEPT)
        own_b(LAST).wait()
        gather_done(LAST)
        tail_load(LAST, late, half_depth)
        arrive(10)
        multiply(LAST, LAST, low, 3, True, raw=True)
        tail_wait(LAST, late, half_depth)
        arrive(11)
        finish(LAST, False, late, half_depth)
        for at in range(count):
            for copy in shared_codes(at, 0, 0):
                copy.wait_recv()
            place = pl.ds(at * TILE, TILE)
            decode(
                shared.at[at, 0],
                shared_scales.at[at, 0],
                row_ref[FIRST, place, :],
                col_ref[FIRST][:, KEPT:],
                out_ref.at[FIRST, place, pl.ds(KEPT, columns - KEPT)],
            )
        for half in range(HALVES):
            extra_copy(half).wait_send()
            for step in range(2):
                shared_copy(step, half).wait_send()
        for index in range(CHUNKS * len(IN)):
            in_copy(index).wait_send()
        for which in (FIRST, LAST):
            gather_sent(which)


def linked_body(
    amplitudes,
    integrals,
    occupied_irrep,
    virtual_order,
    block_irreps,
    occupied_energy,
    virtual_energy,
):
    blocks, virt_local, occ_local, pair_width = amplitudes.shape
    depth, column_width = integrals.shape[1:]
    rows = virt_local * occ_local
    update = pl.pallas_call(
        kernel,
        out_shape=(
            pltpu.VMEM((blocks, 8 * rows, column_width), jnp.float32),
            jax.ShapeDtypeStruct((blocks + 2, 8, rows, pair_width), jnp.bfloat16),
        ),
        in_specs=[pl.BlockSpec(memory_space=pl.ANY)] * 2
        + [
            pl.BlockSpec(memory_space=pltpu.SMEM),
            pl.BlockSpec(memory_space=pltpu.VMEM),
            pl.BlockSpec(memory_space=pltpu.SMEM),
            pl.BlockSpec(memory_space=pltpu.SMEM),
            pl.BlockSpec(memory_space=pltpu.VMEM),
        ],
        out_specs=(pl.BlockSpec(memory_space=pltpu.VMEM), pl.BlockSpec(memory_space=pl.ANY)),
        scratch_shapes=[
            pltpu.VMEM((blocks, pair_width, column_width), jnp.bfloat16),
            pltpu.VMEM((2, TILE // rows, rows, pair_width), jnp.bfloat16),
            pltpu.VMEM((8, rows, depth), jnp.bfloat16),
            pltpu.VMEM((8 * rows // TILE, TILE // 2, column_width), jnp.int32),
            pltpu.VMEM((8 * rows // TILE, GROUPS, column_width), jnp.float32),
            pltpu.VMEM((blocks, 8 * rows, 1), jnp.float32),
            pltpu.VMEM((blocks, 1, column_width), jnp.float32),
            pltpu.VMEM((pair_width, column_width - KEPT), jnp.bfloat16),
            pltpu.VMEM((pair_width, column_width - KEPT), jnp.bfloat16),
            pltpu.VMEM((8 * rows // TILE, 2, TILE // 2, column_width - KEPT), jnp.int32),
            pltpu.VMEM((8 * rows // TILE, 2, GROUPS, column_width - KEPT), jnp.float32),
            pltpu.SemaphoreType.DMA((CHUNKS * len(MID),)),
            pltpu.SemaphoreType.DMA((CHUNKS * len(MID),)),
            pltpu.SemaphoreType.DMA((CHUNKS * len(OUT),)),
            pltpu.SemaphoreType.DMA((CHUNKS * len(OUT),)),
            pltpu.SemaphoreType.DMA((2 * 8 * rows // TILE,)),
            pltpu.SemaphoreType.DMA((2 * 8 * rows // TILE,)),
            pltpu.SemaphoreType.DMA((CHUNKS * len(IN) + 3 * HALVES,)),
            pltpu.SemaphoreType.DMA((CHUNKS * len(IN) + 3 * HALVES,)),
            pltpu.SemaphoreType.DMA((10 * (blocks + 1) + 2,)),
            pltpu.SemaphoreType.DMA((10 * (blocks + 1) + 2,)),
            pltpu.SemaphoreType.DMA((blocks,)),
            pltpu.SemaphoreType.DMA((2, TILE // rows)),
            pltpu.SemaphoreType.DMA((8,)),
            pltpu.SemaphoreType.DMA((4,)),
            pltpu.SemaphoreType.DMA((4,)),
            pltpu.SemaphoreType.DMA((8,)),
            pltpu.SemaphoreType.DMA((8,)),
        ],
        compiler_params=pltpu.CompilerParams(
            collective_id=0, has_side_effects=True, vmem_limit_bytes=46 * 2**20
        ),
    )(
        amplitudes.reshape(blocks, rows, pair_width),
        integrals,
        occupied_irrep,
        virtual_order,
        block_irreps,
        occupied_energy,
        virtual_energy,
    )[0]
    return update.reshape(blocks, 8 * virt_local, occ_local, column_width)


def solution(mesh):
    placed = (P(None, "pair", "row", None), P(None, "row", "pair"), P(), P(), P(), P(), P())
    linked = mesh.shape["pair"] == 8 and mesh.shape["row"] == 4
    return jax.shard_map(
        linked_body if linked else body,
        mesh=mesh,
        in_specs=placed,
        out_specs=P(None, None, "row", "pair"),
        check_vma=False,
    )
```

```python
import jax
import jax.numpy as jnp
from jax import lax
from jax.experimental import pallas as pl
from jax.experimental.pallas import tpu as pltpu
from jax.sharding import PartitionSpec as P

VIRG = 160


def shift_table(occupied_irrep, virtual_order, block_irreps, occupied_energy, virtual_energy):
    count_virt = virtual_energy.shape[0]
    orbital_ids = jnp.arange(count_virt, dtype=jnp.int32)
    matches = virtual_order[:, None] == orbital_ids[None, :]
    slot_energy = jnp.sum(jnp.where(matches, virtual_energy[None, :], jnp.float32(0.0)), axis=1)
    irrep_count = count_virt // VIRG
    energy_grid = slot_energy.reshape(irrep_count, VIRG)
    pair_irrep = jnp.bitwise_xor(block_irreps[:, None], occupied_irrep[None, :])
    irrep_ids = jnp.arange(irrep_count, dtype=jnp.int32)
    chosen = pair_irrep[:, None, None, :] == irrep_ids[None, :, None, None]
    picked = jnp.sum(jnp.where(chosen, energy_grid[None, :, :, None], jnp.float32(0.0)), axis=1)
    return picked - occupied_energy[None, None, :]


def body(
    amplitudes,
    integrals,
    occupied_irrep,
    virtual_order,
    block_irreps,
    occupied_energy,
    virtual_energy,
):
    block_count, virt_local, occ_local, pair_width = amplitudes.shape
    column_width = integrals.shape[2]
    shift = shift_table(
        occupied_irrep, virtual_order, block_irreps, occupied_energy, virtual_energy
    )
    occ_start = lax.axis_index("row") * occ_local
    col_start = lax.axis_index("pair") * column_width
    results = []
    for block in range(block_count):
        whole_rows = lax.all_gather(integrals[block], "row", axis=0, tiled=True)
        piece = lax.all_gather(amplitudes[block], "pair", axis=0, tiled=True)
        flat = piece.reshape(piece.shape[0] * piece.shape[1], piece.shape[2])
        product = jnp.dot(flat, whole_rows, preferred_element_type=jnp.float32)
        cycle_term = product.reshape(piece.shape[0], piece.shape[1], whole_rows.shape[1])
        row_shift = lax.dynamic_slice_in_dim(shift[block], occ_start, occ_local, 1)
        col_shift = lax.dynamic_slice_in_dim(
            shift[block].reshape(pair_width), col_start, column_width, 0
        )
        denominator = row_shift[:, :, None] + col_shift[None, None, :]
        results.append(cycle_term / denominator)
    return jnp.stack(results)


CHUNKS = 4
HALVES = 2
TILE = 320
GROUPS = 8
HELPED, FIRST, LAST = 0, 1, 2
EXTRA, SHARED = 3, 4
KEPT = 512
MID = [(LAST, "own"), (HELPED, "own"), (HELPED, "near"), (FIRST, "own"), (FIRST, "near"), (LAST, "near")]
OUT = [(LAST, "own"), (LAST, "mid"), (FIRST, "own"), (FIRST, "mid"), (FIRST, "far"), (LAST, "far")]
IN = [HELPED, FIRST, LAST]
MESH = pl.DeviceIdType.MESH


def encode(total, coded_ref, scale_ref):
    group = TILE // GROUPS
    for part in range(GROUPS // 2):
        words = []
        for place in (part, part + GROUPS // 2):
            values = total[place * group : (place + 1) * group]
            top = jnp.maximum(jnp.max(jnp.abs(values), axis=0, keepdims=True), jnp.float32(1e-33))
            scale_ref[place : place + 1, :] = top * jnp.float32(1.0 / 32767.0)
            words.append(jnp.round(values * (jnp.float32(32767.0) / top)).astype(jnp.int32))
        coded_ref[part * group : (part + 1) * group, :] = (words[0] << 16) | (words[1] & 0xFFFF)


def decode(coded_ref, scale_ref, row_shift, col_shift, out_ref):
    group = TILE // GROUPS
    for part in range(GROUPS // 2):
        words = coded_ref[part * group : (part + 1) * group, :]
        for place, values in ((part, words >> 16), (part + GROUPS // 2, (words << 16) >> 16)):
            inside = slice(place * group, (place + 1) * group)
            total = values.astype(jnp.float32) * scale_ref[place : place + 1, :]
            out_ref[inside, :] = total / (row_shift[inside, :] + col_shift)


def kernel(
    a_ref, b_ref, irrep_ref, order_ref, block_ref, occupied_ref, virtual_ref, out_ref, all_a,
    all_b, tiles, tail, coded, scales, row_ref, col_ref, aside,
    beside, shared, shared_scales,
    mid_send, mid_recv, out_send, out_recv, code_send, code_recv, in_send, in_recv, p_send, p_recv,
    own_sem, tile_sem, tail_sem, beside_send, beside_recv, shared_send, shared_recv,
):
    blocks, a_rows, _ = a_ref.shape
    depth, columns = b_ref.shape[1:]
    chunk, half_depth = depth // CHUNKS, depth // HALVES
    pieces = all_a.shape[1]
    group = TILE // a_rows
    count = pieces // group
    pair = lax.axis_index("pair")
    row = lax.axis_index("row")
    near = row ^ 1
    across = 3 - row
    far = across ^ 1
    is_inner = (row == 1) | (row == 2)

    barrier = pltpu.get_barrier_semaphore()
    friends = [(pair, near), (pair ^ 2, near), (pair, across)] + [(pair ^ step, row) for step in (1, 2, 4)]
    for friend in friends:
        pl.semaphore_signal(barrier, inc=1, device_id=friend, device_id_type=MESH)
    pl.semaphore_wait(barrier, len(friends))

    def remote(source, goal, send, recv, place, device):
        return pltpu.make_async_remote_copy(
            src_ref=source,
            dst_ref=goal,
            send_sem=send.at[place],
            recv_sem=recv.at[place],
            device_id=device,
            device_id_type=MESH,
        )

    def b_copy(block, slot, turn, own, send, recv, place, device, width=columns):
        kept = pl.ds(0, width)
        offset = jnp.where(slot == 0, CHUNKS - 1 - turn, turn) * chunk
        goal = all_b.at[block, pl.ds(pl.multiple_of(slot * depth + offset, chunk), chunk), kept]
        source = b_ref.at[block, pl.ds(pl.multiple_of(offset, chunk), chunk), kept] if own else goal
        return remote(source, goal, send, recv, place, device)

    def mid_copy(index):
        block, kind = MID[index // CHUNKS]
        slot = row if kind == "own" else near
        return b_copy(
            block, slot, index % CHUNKS, kind == "own", mid_send, mid_recv, index, (pair, across)
        )

    def out_copy(index):
        block, kind = OUT[index // CHUNKS]
        slot = {"own": row, "mid": across, "far": far}[kind]
        return b_copy(
            block, slot, index % CHUNKS, kind == "own", out_send, out_recv, index, (pair, near),
            KEPT if block == FIRST else columns,
        )

    def in_copy(index):
        return b_copy(
            IN[index // CHUNKS], row, index % CHUNKS, True, in_send, in_recv, index, (pair, near)
        )

    def code_copies(at):
        return [
            remote(coded.at[at], coded.at[at], code_send, code_recv, 2 * at, (pair, near)),
            remote(scales.at[at], scales.at[at], code_send, code_recv, 2 * at + 1, (pair, near)),
        ]

    def piece(half):
        size = a_rows // HALVES
        return pl.ds(half * size, size)

    def extra_copy(half):
        part = piece(half)
        return remote(
            a_ref.at[HELPED, part],
            all_a.at[EXTRA, pair, part],
            in_send,
            in_recv,
            CHUNKS * len(IN) + half,
            (pair, near),
        )

    def shared_copy(step, half):
        part = piece(half)
        owner = pair ^ (4 * step)
        source = a_ref.at[FIRST, part] if step == 0 else all_a.at[FIRST, owner, part]
        return remote(
            source,
            all_a.at[SHARED, owner, part],
            in_send,
            in_recv,
            CHUNKS * len(IN) + HALVES * (1 + step) + half,
            (pair, near),
        )

    def shared_core(step):
        owner = pair ^ (4 * step)
        source = all_a.at[SHARED, owner]
        return remote(source, source, p_send, p_recv, 10 * SHARED + step, (pair ^ 1, row))

    def beside_copy(slot, place):
        part = pl.ds(pl.multiple_of(slot * depth, depth), depth)
        return remote(aside.at[part], beside.at[part], beside_send, beside_recv, place, (pair ^ 2, row))

    def beside_start(slot, place):
        part = pl.ds(pl.multiple_of(slot * depth, depth), depth)
        aside[part, :] = all_b[FIRST, part, KEPT:]
        beside_copy(slot, place).start()

    def shared_codes(at, turn, side):
        device = (pair ^ (2 * side), near)
        return [
            pltpu.make_async_remote_copy(
                src_ref=held.at[at, side],
                dst_ref=held.at[at, 0],
                send_sem=shared_send.at[4 * turn + 2 * side + place],
                recv_sem=shared_recv.at[2 * at + place],
                device_id=device,
                device_id_type=MESH,
            )
            for place, held in enumerate((shared, shared_scales))
        ]

    def own_part(which):
        return all_a.at[EXTRA, pair] if which == EXTRA else a_ref.at[which]

    def plane_copy(which, step, half):
        part = piece(half)
        return remote(
            own_part(which).at[part],
            all_a.at[which, pair, part],
            p_send,
            p_recv,
            10 * which + 2 * (step - 1) + half,
            (pair ^ (2 * step), row),
        )

    def forward_copy(which, step):
        part = piece(step - 1)
        bit = 2 if which == LAST else 2 * step
        return remote(
            all_a.at[which, pair ^ bit, part],
            all_a.at[which, pair ^ bit, part],
            p_send,
            p_recv,
            10 * which + 3 + step,
            (pair ^ (6 - bit), row),
        )

    def core_copy(which, step):
        owner = pair ^ (2 * step)
        return remote(
            own_part(which) if step == 0 else all_a.at[which, owner],
            all_a.at[which, owner],
            p_send,
            p_recv,
            10 * which + 6 + step,
            (pair ^ 1, row),
        )

    def gather_start(which):
        plane_copy(which, 1, 0).start()
        plane_copy(which, 2, 1).start()
        plane_copy(which, 1, 1).start()
        plane_copy(which, 2, 0).start()
        core_copy(which, 0).start()

    def gather_forward(which):
        plane_copy(which, 1, 0).wait_recv()
        forward_copy(which, 1).start()
        plane_copy(which, 1 if which == LAST else 2, 1).wait_recv()
        forward_copy(which, 2).start()

    def gather_share(which):
        if which == LAST:
            core_copy(which, 1).start()
            for half in range(HALVES):
                plane_copy(which, 2, half).wait_recv()
            core_copy(which, 2).start()
            return
        for step in (1, 2):
            plane_copy(which, step, 2 - step).wait_recv()
            core_copy(which, step).start()

    def gather_corner(which):
        for step in (1, 2):
            forward_copy(which, step).wait_recv()
        core_copy(which, 3).start()

    def gather_done(which, steps=(0, 1, 2, 3)):
        for step in steps:
            core_copy(which, step).wait_recv()

    def gather_sent(which):
        for step in (1, 2):
            for half in range(HALVES):
                plane_copy(which, step, half).wait_send()
            forward_copy(which, step).wait_send()
        for step in range(4):
            core_copy(which, step).wait_send()

    def own_b(block):
        return pltpu.make_async_copy(
            b_ref.at[block],
            all_b.at[block, pl.ds(pl.multiple_of(row * depth, depth), depth)],
            own_sem.at[block],
        )

    def fill_shifts():
        count_virt = order_ref.shape[0]
        lanes = 128

        def iota(shape, dim):
            return lax.broadcasted_iota(jnp.int32, shape, dim)

        def pick(match, values, axis):
            chosen = jnp.where(match, values, jnp.float32(0.0))
            return jnp.sum(chosen, axis=axis, keepdims=True)

        def upright(line):
            same = iota((lanes, lanes), 0) == iota((lanes, lanes), 1)
            return jnp.concatenate(
                [
                    pick(same, line[:, start : start + lanes], 1)
                    for start in range(0, count_virt, lanes)
                ],
                axis=0,
            )

        def spread(index, scalars):
            chosen = jnp.full(index.shape, scalars[0])
            for place, scalar in enumerate(scalars[1:], 1):
                chosen = jnp.where(index == place, scalar, chosen)
            return chosen

        energies = upright(virtual_ref[...].reshape(1, count_virt))
        order = order_ref[...].reshape(1, count_virt)
        line = jnp.zeros((1, count_virt), jnp.float32)
        for start in range(0, count_virt, lanes):
            match = iota((lanes, count_virt), 0) + start == order
            line += pick(match, energies[start : start + lanes], 0)
        stand = upright(line)
        occ_local = irrep_ref.shape[0] // 4
        place = iota((1, columns), 1)
        which = lax.rem(place, irrep_ref.shape[0])
        irreps = spread(which, [irrep_ref[i] for i in range(irrep_ref.shape[0])])
        occupied = spread(which, [occupied_ref[i] for i in range(irrep_ref.shape[0])])
        virt = place // irrep_ref.shape[0] + pair * (columns // irrep_ref.shape[0])
        for block in range(blocks):
            goal = (irreps ^ block_ref[block]) * VIRG + virt
            total = jnp.zeros((1, columns), jnp.float32)
            for start in range(0, count_virt, 2 * lanes):
                match = iota((2 * lanes, columns), 0) + start == goal
                total += pick(match, stand[start : start + 2 * lanes], 0)
            col_ref[block] = total - occupied

        place = iota((lanes, 1), 0)
        which = lax.rem(place, occ_local)
        irreps = spread(which, [irrep_ref[row * occ_local + i] for i in range(occ_local)])
        occupied = spread(which, [occupied_ref[row * occ_local + i] for i in range(occ_local)])

        def strip(turn, carry):
            start = pl.multiple_of(turn * lanes, lanes)
            for block in range(blocks):
                goal = (irreps ^ block_ref[block]) * VIRG + (place + start) // occ_local
                match = iota((lanes, count_virt), 1) == goal
                row_ref[block, pl.ds(start, lanes), :] = pick(match, line, 1) - occupied
            return carry

        lax.fori_loop(0, row_ref.shape[1] // lanes, strip, 0)

    low, high = row // 2, 3 * (1 - row // 2)
    early = pl.multiple_of(high * depth + jnp.where(high == 0, half_depth, 0), half_depth)
    late = pl.multiple_of(high * depth + jnp.where(high == 0, 0, half_depth), half_depth)

    def fetch(which, owner, goal, sem, span=None):
        def start(source):
            source = source if span is None else source.at[:, span]
            pltpu.make_async_copy(source, goal, sem).start()

        if which >= EXTRA:
            start(all_a.at[which, owner])
        else:

            @pl.when(owner == pair)
            def _():
                start(a_ref.at[which])

            @pl.when(owner != pair)
            def _():
                start(all_a.at[which, owner])

    def tile_load(which, at, slot):
        for place in range(group):
            fetch(which, at * group + place, tiles.at[slot, place], tile_sem.at[slot, place])

    def tail_load(which, first, size):
        for owner in range(pieces):
            goal = tail.at[owner, :, pl.ds(0, size)]
            fetch(which, owner, goal, tail_sem.at[owner], pl.ds(first, size))

    def tail_wait(which, first, size):
        for owner in range(pieces):
            goal = tail.at[owner, :, pl.ds(0, size)]
            pltpu.make_async_copy(
                all_a.at[which, owner, :, pl.ds(first, size)], goal, tail_sem.at[owner]
            ).wait()

    def product(left, block, start, size, width=columns):
        right = all_b[block, pl.ds(start, size), :width]
        return jnp.dot(left.reshape(TILE, size), right, preferred_element_type=jnp.float32)

    def divide(total, block, place):
        return total / (row_ref[block, place, :] + col_ref[block][:, : total.shape[1]])

    def share(at, turn):
        tile_load(SHARED, at, 0)
        for place in range(group):
            pltpu.make_async_copy(
                all_a.at[SHARED, at * group + place], tiles.at[0, place], tile_sem.at[0, place]
            ).wait()
        for side in range(2):

            def add(part, total):
                span = pl.ds(pl.multiple_of(part * depth, depth), depth)
                right = beside[span, :] if side else aside[span, :]
                left = tiles[0, :, :, span].reshape(TILE, depth)
                return total + jnp.dot(left, right, preferred_element_type=jnp.float32)

            total = lax.fori_loop(0, 4, add, jnp.zeros((TILE, columns - KEPT), jnp.float32))
            encode(total, shared.at[at, side], shared_scales.at[at, side])
            for copy in shared_codes(at, turn, side):
                copy.start()

    def multiply(which, block, first, parts, rest=False, width=columns, span=(0, count), raw=False):
        home = pair // group
        tile_load(which, home ^ span[0], span[0] % 2)

        def step(turn, carry):
            slot = turn % 2
            at = home ^ turn

            @pl.when(turn + 1 < span[1])
            def _():
                tile_load(which, home ^ (turn + 1), 1 - slot)

            for place in range(group):
                pltpu.make_async_copy(
                    all_a.at[which, at * group + place], tiles.at[slot, place], tile_sem.at[slot, place]
                ).wait()

            def add(part, total):
                start = pl.multiple_of((first + part) * depth, depth)
                return total + product(
                    tiles[slot, :, :, pl.ds(start, depth)], block, start, depth, width
                )

            total = lax.fori_loop(0, parts, add, jnp.zeros((TILE, width), jnp.float32))
            if rest:
                total += product(tiles[slot, :, :, pl.ds(early, half_depth)], block, early, half_depth)
            place = pl.ds(pl.multiple_of(at * TILE, TILE), TILE)
            out_ref[block, place, :width] = total if raw else divide(total, block, place)
            return carry

        lax.fori_loop(span[0], span[1], step, 0)

    def finish(block, code, first, size):
        def step(at, carry):
            place = pl.ds(pl.multiple_of(at * TILE, TILE), TILE)
            left = tail[pl.ds(at * group, group), :, :size]
            total = out_ref[block, place, :] + product(left, block, first, size)
            if code:
                encode(total, coded.at[at], scales.at[at])
                for copy in code_copies(at):
                    copy.start()
            else:
                out_ref[block, place, :] = divide(total, block, place)
            return carry

        lax.fori_loop(0, count, step, 0)

    @pl.when(is_inner)
    def _():
        def arrive(turn):
            for step in range(turn * CHUNKS // 2, (turn + 1) * CHUNKS // 2):
                mid_copy(step).wait_recv()
                block, kind = MID[step // CHUNKS]
                entry = (block, "mid" if kind == "own" else "far")
                if entry in OUT:
                    out_copy(CHUNKS * OUT.index(entry) + step % CHUNKS).start()
                later = step + CHUNKS
                if later < CHUNKS * len(MID):
                    block, kind = MID[later // CHUNKS]
                    if kind == "near":
                        in_copy(CHUNKS * IN.index(block) + later % CHUNKS).wait_recv()
                    mid_copy(later).start()

        def fill(block, half):
            for step in range(half * CHUNKS // 2, (half + 1) * CHUNKS // 2):
                out_copy(CHUNKS * OUT.index((block, "own")) + step).start()

        for step in range(CHUNKS):
            mid_copy(step).start()
            out_copy(step).start()
        gather_start(HELPED)
        for block in (HELPED, FIRST, LAST):
            own_b(block).start()
        fill_shifts()
        arrive(0)
        arrive(1)
        for half in range(HALVES):
            extra_copy(half).wait_recv()
        gather_start(EXTRA)
        fill(FIRST, 0)
        arrive(2)
        fill(FIRST, 1)
        own_b(FIRST).wait()
        beside_start(row, 0)
        arrive(3)
        gather_forward(EXTRA)
        gather_forward(HELPED)
        gather_share(EXTRA)
        gather_share(HELPED)
        gather_start(FIRST)
        own_b(HELPED).wait()
        gather_done(EXTRA, (0, 1, 2))
        multiply(EXTRA, HELPED, low, 3, span=(0, 3), raw=True)
        arrive(4)
        gather_corner(EXTRA)
        gather_done(EXTRA, (3,))
        begin = pl.multiple_of(high * depth, depth)
        tail_load(EXTRA, begin, depth)
        multiply(EXTRA, HELPED, low, 3, span=(3, 4), raw=True)
        tail_wait(EXTRA, begin, depth)
        arrive(5)
        finish(HELPED, True, begin, depth)
        gather_corner(HELPED)
        arrive(6)
        gather_forward(FIRST)
        gather_start(LAST)
        gather_done(HELPED)
        multiply(HELPED, HELPED, 0, 4)
        arrive(7)
        gather_share(FIRST)
        beside_start(near, 1)
        beside_start(across, 2)
        arrive(8)
        gather_corner(FIRST)
        arrive(9)
        beside_start(far, 3)
        gather_done(FIRST)
        multiply(FIRST, FIRST, 0, 4)
        gather_forward(LAST)
        arrive(10)
        gather_share(LAST)
        for half in range(HALVES):
            shared_copy(0, half).wait_recv()
        shared_core(0).start()
        own_b(LAST).wait()
        gather_done(LAST, (0, 1, 2))
        multiply(LAST, LAST, low, 3, True, span=(0, 3), raw=True)
        for place in range(4):
            beside_copy(row, place).wait_recv()
        shared_core(0).wait_recv()
        share(pair // group, 0)
        arrive(11)
        for half in range(HALVES):
            shared_copy(1, half).wait_recv()
        shared_core(1).start()
        gather_corner(LAST)
        gather_done(LAST, (3,))
        tail_load(LAST, late, half_depth)
        shared_core(1).wait_recv()
        share((pair ^ 4) // group, 1)
        multiply(LAST, LAST, low, 3, True, span=(3, 4), raw=True)
        tail_wait(LAST, late, half_depth)
        finish(LAST, False, late, half_depth)
        for index in range(CHUNKS * len(MID)):
            mid_copy(index).wait_send()
        for index in range(CHUNKS * len(OUT)):
            out_copy(index).wait_send()
        for at in range(count):
            for copy in code_copies(at):
                copy.wait_send()
        for which in (FIRST, EXTRA, HELPED, LAST):
            gather_sent(which)
        for step in range(2):
            shared_core(step).wait_send()
            for side in range(2):
                for copy in shared_codes((pair ^ (4 * step)) // group, step, side):
                    copy.wait_send()
        for place, slot in enumerate((row, near, across, far)):
            beside_copy(slot, place).wait_send()

    @pl.when(jnp.logical_not(is_inner))
    def _():
        def arrive(turn):
            for step in range(turn * CHUNKS // 2, (turn + 1) * CHUNKS // 2):
                out_copy(step).wait_recv()
                if step < CHUNKS * len(IN):
                    in_copy(step).start()

        for half in range(HALVES):
            extra_copy(half).start()
        gather_start(FIRST)
        for block in (FIRST, LAST):
            own_b(block).start()
        fill_shifts()
        arrive(0)
        gather_forward(FIRST)
        arrive(1)
        gather_share(FIRST)
        gather_start(LAST)
        arrive(2)
        gather_corner(FIRST)
        arrive(3)
        gather_forward(LAST)
        arrive(4)
        gather_share(LAST)
        arrive(5)
        gather_corner(LAST)
        for at in range(count):
            for copy in code_copies(at):
                copy.wait_recv()
            if at < HALVES:
                shared_copy(0, at).start()
            place = pl.ds(at * TILE, TILE)
            decode(
                coded.at[at],
                scales.at[at],
                row_ref[HELPED, place, :],
                col_ref[HELPED],
                out_ref.at[HELPED, place],
            )
        arrive(6)
        shared_copy(1, 0).start()
        arrive(7)
        shared_copy(1, 1).start()
        arrive(8)
        arrive(9)
        own_b(FIRST).wait()
        gather_done(FIRST)
        multiply(FIRST, FIRST, 0, 4, width=KEPT)
        own_b(LAST).wait()
        gather_done(LAST)
        tail_load(LAST, late, half_depth)
        arrive(10)
        multiply(LAST, LAST, low, 3, True, raw=True)
        tail_wait(LAST, late, half_depth)
        arrive(11)
        finish(LAST, False, late, half_depth)
        for at in range(count):
            for copy in shared_codes(at, 0, 0):
                copy.wait_recv()
            place = pl.ds(at * TILE, TILE)
            decode(
                shared.at[at, 0],
                shared_scales.at[at, 0],
                row_ref[FIRST, place, :],
                col_ref[FIRST][:, KEPT:],
                out_ref.at[FIRST, place, pl.ds(KEPT, columns - KEPT)],
            )
        for half in range(HALVES):
            extra_copy(half).wait_send()
            for step in range(2):
                shared_copy(step, half).wait_send()
        for index in range(CHUNKS * len(IN)):
            in_copy(index).wait_send()
        for which in (FIRST, LAST):
            gather_sent(which)


def linked_body(
    amplitudes,
    integrals,
    occupied_irrep,
    virtual_order,
    block_irreps,
    occupied_energy,
    virtual_energy,
):
    blocks, virt_local, occ_local, pair_width = amplitudes.shape
    depth, column_width = integrals.shape[1:]
    rows = virt_local * occ_local
    update = pl.pallas_call(
        kernel,
        out_shape=(
            pltpu.VMEM((blocks, 8 * rows, column_width), jnp.float32),
            jax.ShapeDtypeStruct((blocks + 2, 8, rows, pair_width), jnp.bfloat16),
        ),
        in_specs=[pl.BlockSpec(memory_space=pl.ANY)] * 2
        + [
            pl.BlockSpec(memory_space=pltpu.SMEM),
            pl.BlockSpec(memory_space=pltpu.VMEM),
            pl.BlockSpec(memory_space=pltpu.SMEM),
            pl.BlockSpec(memory_space=pltpu.SMEM),
            pl.BlockSpec(memory_space=pltpu.VMEM),
        ],
        out_specs=(pl.BlockSpec(memory_space=pltpu.VMEM), pl.BlockSpec(memory_space=pl.ANY)),
        scratch_shapes=[
            pltpu.VMEM((blocks, pair_width, column_width), jnp.bfloat16),
            pltpu.VMEM((2, TILE // rows, rows, pair_width), jnp.bfloat16),
            pltpu.VMEM((8, rows, depth), jnp.bfloat16),
            pltpu.VMEM((8 * rows // TILE, TILE // 2, column_width), jnp.int32),
            pltpu.VMEM((8 * rows // TILE, GROUPS, column_width), jnp.float32),
            pltpu.VMEM((blocks, 8 * rows, 1), jnp.float32),
            pltpu.VMEM((blocks, 1, column_width), jnp.float32),
            pltpu.VMEM((pair_width, column_width - KEPT), jnp.bfloat16),
            pltpu.VMEM((pair_width, column_width - KEPT), jnp.bfloat16),
            pltpu.VMEM((8 * rows // TILE, 2, TILE // 2, column_width - KEPT), jnp.int32),
            pltpu.VMEM((8 * rows // TILE, 2, GROUPS, column_width - KEPT), jnp.float32),
            pltpu.SemaphoreType.DMA((CHUNKS * len(MID),)),
            pltpu.SemaphoreType.DMA((CHUNKS * len(MID),)),
            pltpu.SemaphoreType.DMA((CHUNKS * len(OUT),)),
            pltpu.SemaphoreType.DMA((CHUNKS * len(OUT),)),
            pltpu.SemaphoreType.DMA((2 * 8 * rows // TILE,)),
            pltpu.SemaphoreType.DMA((2 * 8 * rows // TILE,)),
            pltpu.SemaphoreType.DMA((CHUNKS * len(IN) + 3 * HALVES,)),
            pltpu.SemaphoreType.DMA((CHUNKS * len(IN) + 3 * HALVES,)),
            pltpu.SemaphoreType.DMA((10 * (blocks + 1) + 2,)),
            pltpu.SemaphoreType.DMA((10 * (blocks + 1) + 2,)),
            pltpu.SemaphoreType.DMA((blocks,)),
            pltpu.SemaphoreType.DMA((2, TILE // rows)),
            pltpu.SemaphoreType.DMA((8,)),
            pltpu.SemaphoreType.DMA((4,)),
            pltpu.SemaphoreType.DMA((4,)),
            pltpu.SemaphoreType.DMA((8,)),
            pltpu.SemaphoreType.DMA((8,)),
        ],
        compiler_params=pltpu.CompilerParams(
            collective_id=0, has_side_effects=True, vmem_limit_bytes=46 * 2**20
        ),
    )(
        amplitudes.reshape(blocks, rows, pair_width),
        integrals,
        occupied_irrep,
        virtual_order,
        block_irreps,
        occupied_energy,
        virtual_energy,
    )[0]
    return update.reshape(blocks, 8 * virt_local, occ_local, column_width)


def solution(mesh):
    placed = (P(None, "pair", "row", None), P(None, "row", "pair"), P(), P(), P(), P(), P())
    linked = mesh.shape["pair"] == 8 and mesh.shape["row"] == 4
    return jax.shard_map(
        linked_body if linked else body,
        mesh=mesh,
        in_specs=placed,
        out_specs=P(None, None, "row", "pair"),
        check_vma=False,
    )
```
